256 devices in a mesh: seq: 16 (over z, y_lo), res: 16 (over y_hi, x, core).
Axes of the slice: x: 4, y: 4 (y_hi: 2, y_lo: 2; y = y_hi * 2 + y_lo), z: 8, core: 2. Of those that a mesh axis runs over, the one named last changes fastest.
Arguments:
- target_alignment_matrix: float32 [1024, 128, 256], P('seq', 'res'), may hold values from -6 to 6
- source_alignment_matrix: float32 [1024, 128, 256], P('seq', 'res'), may hold values from -6 to 6
- source_mapping_matrix: float32 [256, 32], replicated, may hold values from -0.375 to 0.375
- target_mapping_matrix: float32 [256, 32], replicated, may hold values from -0.375 to 0.375
- final_mapping_matrix: float32 [1024, 128], replicated, may hold values from -6 to 6
- edge_offset_vector: float32 [128], replicated, may hold values from -3 to 3
- edge_delta_cotangent: float32 [128, 128, 128], P('seq', 'res'), may hold values from -6 to 6
Outputs:
- edge_delta_result: float32 [128, 128, 128], P('seq', 'res')
- grad_cols: float32 [1024, 128, 256], P('seq', 'res')
- grad_rows: float32 [1024, 128, 256], P('seq', 'res')
- grad_left: float32 [256, 32], replicated
- grad_right: float32 [256, 32], replicated
- grad_proj: float32 [1024, 128], replicated
- grad_bias: float32 [128], replicated
The draws below stay inside these ranges and needn't reach their ends.
All inputs are finite; a program needn't handle non-finite values.
Results may differ from the reference program's by a relative error of at most 0.00013.
Values sent between devices are 32-bit elements; how exact they have to be, the bound alone decides.
A program may use at most 64 MiB of HBM per device.

```python
import jax
import jax.numpy as jnp
from jax import lax

ALIGN_FEATURES = 256
HIDDEN_WIDTH = 32
EDGE_FEATURES = 128
SOURCE_AMINOS = 128
ALIGN_MEMBERS = 1024
TARGET_AMINOS = 128


def levels(rng, shape, cuts, low, high):
    def one(axis_at, parts):
        draws = jax.random.uniform(jax.random.fold_in(jax.random.fold_in(rng, 6), axis_at), (parts,), jnp.float32, low / len(cuts), high / len(cuts))
        return jnp.repeat(jnp.exp(draws), shape[axis_at] // parts).reshape((-1,) + (1,) * (len(shape) - axis_at - 1))

    factor_of = one(*cuts[0])
    for cut in cuts[1:]:
        factor_of = factor_of * one(*cut)
    return factor_of


def scatter_about(stream_key, dims, scale, bound, cuts=(), kind=jnp.bfloat16):
    values = jax.random.normal(stream_key, dims, jnp.float32) * scale
    if len(cuts) > 0:
        values = levels(stream_key, dims, cuts, -0.22, 0.18) * values
    return jnp.clip(values, min=-bound, max=bound).astype(kind)


def setup_inputs(seed: int = 0) -> dict:
    streams_of = jax.random.split(jax.random.key(seed), 8)
    return {
        "target_alignment_matrix": scatter_about(streams_of[0], (ALIGN_MEMBERS, TARGET_AMINOS, ALIGN_FEATURES), 1.0, 6.0, ((0, 16), (1, 16)), jnp.float32),
        "source_alignment_matrix": scatter_about(streams_of[1], (ALIGN_MEMBERS, SOURCE_AMINOS, ALIGN_FEATURES), 1.0, 6.0, ((0, 16), (1, 16)), jnp.float32),
        "source_mapping_matrix": scatter_about(streams_of[2], (ALIGN_FEATURES, HIDDEN_WIDTH), ALIGN_FEATURES ** -0.5, 0.375, (), jnp.float32),
        "target_mapping_matrix": scatter_about(streams_of[3], (ALIGN_FEATURES, HIDDEN_WIDTH), ALIGN_FEATURES ** -0.5, 0.375, (), jnp.float32),
        "final_mapping_matrix": scatter_about(streams_of[4], (HIDDEN_WIDTH * HIDDEN_WIDTH, EDGE_FEATURES), (ALIGN_MEMBERS ** 0.5 * 0.03125), 6.0, (), jnp.float32),
        "edge_offset_vector": scatter_about(streams_of[5], (EDGE_FEATURES,), 0.5, 3.0, (), jnp.float32),
        "edge_delta_cotangent": scatter_about(streams_of[6], (SOURCE_AMINOS, TARGET_AMINOS, EDGE_FEATURES), 1.0, 6.0, ((0, 16), (1, 16)), jnp.float32),
    }


def standardize_features(values):
    average = lax.optimization_barrier(jnp.mean(values, axis=-1, keepdims=True))
    centred = values - average
    inverse = lax.rsqrt(lax.optimization_barrier(jnp.mean(centred * centred, axis=-1, keepdims=True)) + 1e-05)
    return centred * inverse

def evaluate_primal(target_alignment_matrix, source_alignment_matrix, source_mapping_matrix, target_mapping_matrix, final_mapping_matrix, edge_offset_vector):
    exact_arithmetic = lax.Precision.HIGHEST
    source_mapped_vectors = jnp.einsum('uwh,hq->uwq', standardize_features(source_alignment_matrix), source_mapping_matrix, precision=exact_arithmetic)
    target_mapped_vectors = jnp.einsum('iwe,ed->iwd', standardize_features(target_alignment_matrix), target_mapping_matrix, precision=exact_arithmetic)
    tensor_average_block = jnp.einsum('ipu,ihl->phul', source_mapped_vectors, target_mapped_vectors, precision=exact_arithmetic) / source_alignment_matrix.shape[0]
    rows_total = source_mapped_vectors.shape[1]
    cols_total = target_mapped_vectors.shape[1]
    square = source_mapped_vectors.shape[2] * target_mapped_vectors.shape[2]
    flat_rows = tensor_average_block.reshape(rows_total * cols_total, square)
    projected = jnp.dot(flat_rows, final_mapping_matrix, precision=exact_arithmetic) + edge_offset_vector
    return projected.reshape(rows_total, cols_total, final_mapping_matrix.shape[1])

def reference(target_alignment_matrix, source_alignment_matrix, source_mapping_matrix, target_mapping_matrix, final_mapping_matrix, edge_offset_vector, edge_delta_cotangent):
    edge_delta_result, adjoint_mapping = jax.vjp(evaluate_primal, target_alignment_matrix, source_alignment_matrix, source_mapping_matrix, target_mapping_matrix, final_mapping_matrix, edge_offset_vector)
    grads = adjoint_mapping(edge_delta_cotangent)
    return (edge_delta_result, grads[0], grads[1], grads[2], grads[3], grads[4], grads[5])
```

```python
import functools

import jax
import jax.numpy as jnp
from jax import lax
from jax.experimental import pallas as pl
from jax.experimental.pallas import tpu as pltpu
from jax.sharding import PartitionSpec as P

EPS = 1e-05
VMEM = pltpu.MemorySpace.VMEM


def standardize_features(values):
    average = jnp.mean(values, axis=-1, keepdims=True)
    centred = values - average
    inverse = lax.rsqrt(jnp.mean(centred * centred, axis=-1, keepdims=True) + EPS)
    return (centred * inverse, inverse)


def normalize_back(normed, inverse, upstream):
    first = jnp.mean(upstream, axis=-1, keepdims=True)
    second = jnp.mean(upstream * normed, axis=-1, keepdims=True)
    return inverse * (upstream - first - normed * second)


def peer_of(me, step, size):
    return lax.rem(me + step, size)


def greet(axes):
    barrier = pltpu.get_barrier_semaphore()
    total = 0
    for axis in axes:
        size = lax.axis_size(axis)
        me = lax.axis_index(axis)

        def signal(step, _, me=me, size=size, axis=axis):
            pl.semaphore_signal(
                barrier,
                inc=1,
                device_id={axis: peer_of(me, step, size)},
                device_id_type=pl.DeviceIdType.MESH,
            )
            return 0

        lax.fori_loop(1, size, signal, 0)
        total += size - 1
    pl.semaphore_wait(barrier, total)


def exchange(axis, src_of, dst_of, send_sem, recv_sem):
    size = lax.axis_size(axis)
    me = lax.axis_index(axis)

    def copy(step, target, slot):
        return pltpu.make_async_remote_copy(
            src_ref=src_of(target),
            dst_ref=dst_of(slot),
            send_sem=send_sem.at[target],
            recv_sem=recv_sem.at[slot],
            device_id={axis: target},
            device_id_type=pl.DeviceIdType.MESH,
        )

    def start():
        def one(step, _):
            copy(step, peer_of(me, step, size), me).start()
            return 0

        lax.fori_loop(1, size, one, 0)

    def wait_recv():
        def one(step, _):
            peer = peer_of(me, size - step, size)
            copy(step, peer, peer).wait_recv()
            return 0

        lax.fori_loop(1, size, one, 0)

    def wait_send():
        def one(step, _):
            copy(step, peer_of(me, step, size), me).wait_send()
            return 0

        lax.fori_loop(1, size, one, 0)

    return start, wait_recv, wait_send


def rows_of(block, rows):
    return pl.ds(pl.multiple_of(block * rows, rows), rows)


def gather_kernel(left_ref, cot_ref, left_all, cot_all, ssr, rsr, sss, rss):
    res_me = lax.axis_index("res")
    seq_me = lax.axis_index("seq")
    greet(("seq", "res"))
    s1, r1, w1 = exchange(
        "seq", lambda t: cot_ref, lambda k: cot_all.at[rows_of(k, 8)], sss, rss
    )
    s2, r2, w2 = exchange(
        "res", lambda t: left_ref, lambda k: left_all.at[rows_of(k, 8)], ssr, rsr
    )
    s1()
    s2()
    cot_all[rows_of(seq_me, 8), :] = cot_ref[...]
    left_all[rows_of(res_me, 8), :] = left_ref[...]
    r1()
    r2()
    w1()
    w2()


def scatter_kernel(
    edge_ref, grad_ref, edge_out, grad_out, edge_in, grad_in, ssr, rsr, sss, rss
):
    res_me = lax.axis_index("res")
    seq_me = lax.axis_index("seq")
    greet(("seq", "res"))
    s1, r1, w1 = exchange(
        "seq", lambda t: edge_ref.at[rows_of(t, 8)], lambda k: edge_in.at[k], sss, rss
    )
    s2, r2, w2 = exchange(
        "res", lambda t: grad_ref.at[rows_of(t, 8)], lambda k: grad_in.at[k], ssr, rsr
    )
    s1()
    s2()
    edge_in[seq_me] = edge_ref[rows_of(seq_me, 8), :]
    grad_in[res_me] = grad_ref[rows_of(res_me, 8), :]
    r1()
    edge_out[...] = jnp.sum(edge_in[...], axis=0)
    r2()
    grad_out[...] = jnp.sum(grad_in[...], axis=0)
    w1()
    w2()


def reduce_kernel(
    part_ref, out_ref, in1, acc1, in2, acc2, seqs, s1s, r1s, s2s, r2s, s3s, r3s, s4s, r4s
):
    res_me = lax.axis_index("res")
    seq_me = lax.axis_index("seq")
    greet(("seq", "res"))
    start, recv, sent1 = exchange(
        "res", lambda t: part_ref.at[t], lambda k: in1.at[k], s1s, r1s
    )
    start()
    in1[res_me] = part_ref[res_me]
    recv()
    acc1[...] = jnp.sum(in1[...], axis=0)
    start, recv, sent2 = exchange(
        "seq", lambda t: acc1.at[t], lambda k: in2.at[k], s2s, r2s
    )
    start()
    in2[seq_me] = acc1[seq_me]
    recv()
    acc2[...] = jnp.sum(in2[...], axis=0)
    start, recv, sent3 = exchange(
        "seq", lambda t: acc2, lambda k: seqs.at[k], s3s, r3s
    )
    start()
    seqs[seq_me] = acc2[...]
    recv()
    start, recv, sent4 = exchange(
        "res", lambda t: seqs, lambda k: out_ref.at[k], s4s, r4s
    )
    start()
    out_ref[res_me] = seqs[...]
    recv()
    sent1()
    sent2()
    sent3()
    sent4()


def vspec():
    return pl.BlockSpec(memory_space=VMEM)


def dma(n):
    return pltpu.SemaphoreType.DMA((n,))


def call(kernel, outs, operands, scratch, cid):
    return pl.pallas_call(
        kernel,
        out_shape=outs,
        in_specs=[vspec()] * len(operands),
        out_specs=jax.tree.map(lambda _: vspec(), outs),
        scratch_shapes=scratch,
        compiler_params=pltpu.CompilerParams(collective_id=cid, has_side_effects=True),
        name=kernel.__name__,
    )(*operands)


def body(tgt, src, wl, wr, fin, bias, cot):
    hi = lax.Precision.HIGH
    f32 = jnp.float32
    ns = lax.axis_size("seq")
    nr = lax.axis_size("res")
    s, i, c = src.shape
    j = tgt.shape[1]
    hid = wl.shape[1]
    e = fin.shape[1]
    own = cot.shape[0]
    scale = 1.0 / (s * ns)
    rows, row_inv = standardize_features(src)
    cols, col_inv = standardize_features(tgt)
    left = jnp.einsum("sic,ch->ihs", rows, wl, precision=hi)
    right = jnp.einsum("sjc,ck->jsk", cols, wr, precision=hi) * scale
    left_blk = left.reshape(i, hid * s)
    cot_blk = cot.reshape(own, j * e)
    left_all, cot_all = call(
        gather_kernel,
        (
            jax.ShapeDtypeStruct((nr * i, hid * s), f32),
            jax.ShapeDtypeStruct((ns * own, j * e), f32),
        ),
        (left_blk, cot_blk),
        [dma(nr), dma(nr), dma(ns), dma(ns)],
        0,
    )
    fin3 = fin.reshape(hid, hid, e)
    b = jnp.einsum("jsk,hke->hsje", right, fin3, precision=hi).reshape(hid * s, j * e)
    edge_part = jnp.dot(left_all, b, precision=hi)
    grad_part = lax.dot_general(cot_all, b, (((1,), (1,)), ((), ())), precision=hi)
    edge_blk, gls = call(
        scatter_kernel,
        (
            jax.ShapeDtypeStruct((own, j * e), f32),
            jax.ShapeDtypeStruct((i, hid * s), f32),
        ),
        (edge_part, grad_part),
        [
            pltpu.VMEM((ns, own, j * e), f32),
            pltpu.VMEM((nr, i, hid * s), f32),
            dma(nr),
            dma(nr),
            dma(ns),
            dma(ns),
        ],
        1,
    )
    edge = edge_blk.reshape(own, j, e) + bias
    db = lax.dot_general(left_all, cot_all, (((0,), (0,)), ((), ())), precision=hi)
    db4 = db.reshape(hid, s, j, e)
    grad_fin = jnp.einsum("jsk,hsje->hke", right, db4, precision=hi).reshape(hid * hid, e)
    grs = jnp.einsum("hsje,hke->sjk", db4, fin3, precision=hi) * scale
    gls = gls.reshape(i, hid, s)
    grad_wl = jnp.einsum("sic,ihs->ch", rows, gls, precision=hi)
    grad_wr = jnp.einsum("sjc,sjk->ck", cols, grs, precision=hi)
    grad_b = jnp.sum(cot, axis=(0, 1))
    n = ns * nr
    small = jnp.concatenate([grad_wl.reshape(-1), grad_wr.reshape(-1), grad_b])
    small = jnp.pad(small, (0, n * 128 - small.shape[0])).reshape(n, 128)
    big = grad_fin.reshape(n, -1)
    width = big.shape[1] + 128
    pack = jnp.concatenate([big, small], axis=1).reshape(nr, ns, 1, width)
    red = call(
        reduce_kernel,
        jax.ShapeDtypeStruct((nr, ns, 1, width), f32),
        (pack,),
        [
            pltpu.VMEM((nr, ns, 1, width), f32),
            pltpu.VMEM((ns, 1, width), f32),
            pltpu.VMEM((ns, 1, width), f32),
            pltpu.VMEM((1, width), f32),
            pltpu.VMEM((ns, 1, width), f32),
            dma(nr),
            dma(nr),
            dma(ns),
            dma(ns),
            dma(ns),
            dma(ns),
            dma(nr),
            dma(nr),
        ],
        2,
    )
    red = red.reshape(n, width)
    grad_fin = red[:, : width - 128].reshape(hid * hid, e)
    small = red[:, width - 128 :].reshape(-1)
    grad_wl = small[: c * hid].reshape(c, hid)
    grad_wr = small[c * hid : 2 * c * hid].reshape(c, hid)
    grad_b = small[2 * c * hid : 2 * c * hid + e]
    up_rows = jnp.einsum("ihs,ch->sic", gls, wl, precision=hi)
    up_cols = jnp.einsum("sjk,ck->sjc", grs, wr, precision=hi)
    grad_rows = normalize_back(rows, row_inv, up_rows)
    grad_cols = normalize_back(cols, col_inv, up_cols)
    return (edge, grad_cols, grad_rows, grad_wl, grad_wr, grad_fin, grad_b)


def solution(mesh):
    split = P("seq", "res", None)
    in_specs = (split, split, P(), P(), P(), P(), split)
    out_specs = (split, split, split, P(), P(), P(), P())
    return jax.shard_map(body, mesh=mesh, in_specs=in_specs, out_specs=out_specs, check_vma=False)
```

```python
import functools

import jax
import jax.numpy as jnp
from jax import lax
from jax.experimental import pallas as pl
from jax.experimental.pallas import tpu as pltpu
from jax.sharding import PartitionSpec as P

EPS = 1e-05
F32 = jnp.float32
BF16 = jnp.bfloat16
MESH = pl.DeviceIdType.MESH
NN = (((1,), (0,)), ((), ()))
NT = (((1,), (1,)), ((), ()))


def mm(a, b, dims=NN):
    return lax.dot_general(a, b, dims, preferred_element_type=F32)


def split(x):
    high = x.astype(BF16)
    return high, (x - high.astype(F32)).astype(BF16)


def mm3(a, b, dims=NN):
    return mm(a[0], b[0], dims) + (mm(a[0], b[1], dims) + mm(a[1], b[0], dims))


def signal_peers(axes):
    barrier = pltpu.get_barrier_semaphore()
    for axis in axes:
        size = lax.axis_size(axis)
        me = lax.axis_index(axis)

        def signal(step, _, me=me, size=size, axis=axis):
            pl.semaphore_signal(
                barrier,
                inc=1,
                device_id={axis: lax.rem(me + step, size)},
                device_id_type=MESH,
            )
            return 0

        lax.fori_loop(1, size, signal, 0)


def wait_peers(axes):
    total = sum(lax.axis_size(axis) - 1 for axis in axes)
    pl.semaphore_wait(pltpu.get_barrier_semaphore(), total)


class Exchange:
    def __init__(self, axis, src_of, dst_of, send_sem, recv_sem):
        self.axis = axis
        self.size = lax.axis_size(axis)
        self.me = lax.axis_index(axis)
        self.src_of = src_of
        self.dst_of = dst_of
        self.send_sem = send_sem
        self.recv_sem = recv_sem

    def copy(self, target, slot):
        return pltpu.make_async_remote_copy(
            src_ref=self.src_of(target),
            dst_ref=self.dst_of(slot),
            send_sem=self.send_sem.at[target],
            recv_sem=self.recv_sem.at[slot],
            device_id={self.axis: target},
            device_id_type=MESH,
        )

    def each(self, act):
        def one(step, _):
            act(lax.rem(self.me + step, self.size))
            return 0

        lax.fori_loop(1, self.size, one, 0)

    def start(self):
        self.each(lambda peer: self.copy(peer, self.me).start())

    def wait_recv(self):
        self.each(lambda peer: self.copy(peer, peer).wait_recv())

    def wait_send(self):
        self.each(lambda peer: self.copy(peer, self.me).wait_send())


def block(index, rows):
    return pl.ds(pl.multiple_of(index * rows, rows), rows)


def norm_rows(x_ref, normed, inverse, own, depth):
    def one(i, _):
        x = jnp.concatenate(
            [x_ref[pl.ds(i + p * own, depth, stride=2 * own), :] for p in range(2)], axis=1
        )
        centred = x - jnp.mean(x, axis=-1, keepdims=True)
        inv = lax.rsqrt(jnp.mean(centred * centred, axis=-1, keepdims=True) + EPS)
        normed[block(i, depth), :] = centred * inv
        inverse[block(i, depth), :] = inv
        return 0

    lax.fori_loop(0, own, one, 0)


def norm_back(upstream, normed, inverse, out_ref, own, depth):
    for i in range(own):
        rows = slice(i * depth, (i + 1) * depth)
        u = upstream[rows, :]
        y = normed[rows, :]
        first = jnp.mean(u, axis=-1, keepdims=True)
        second = jnp.mean(u * y, axis=-1, keepdims=True)
        g = inverse[rows, :] * (u - first - y * second)
        for p in range(2):
            lanes = slice(p * 128, (p + 1) * 128)
            out_ref[pl.ds(i + p * own, depth, stride=2 * own), :] = g[:, lanes]


def kernel(
    src, tgt, wl_t, wr_t, fin, bias, cot,
    edge_out, cols_out, rows_out, fin_out, gl_out, gr_out, gb_out,
    xs, xs_inv, xt, xt_inv, turn, left_blk, left_all, left_h, left_l, lt_h, lt_l,
    cot_blk, cot_all, cot_h, cot_l, fin_h, fin_l, b_h, b_l,
    gls_part, gls_in, edge_part, edge_in, db_h, db_l, acc64, acc32, grs_ref, up,
    big, big_in, small, small_in, acc1, in2, acc2, seqs, red,
    s_cot, r_cot, s_left, r_left, s_gls, r_gls, s_edge, r_edge,
    s_big, r_big, s_small, r_small, s_p2, r_p2, s_p3, r_p3, s_p4, r_p4,
    *, own, depth, hid, wide,
):
    nr = lax.axis_size("res")
    ns = lax.axis_size("seq")
    res_me = lax.axis_index("res")
    seq_me = lax.axis_index("seq")
    scale = 1.0 / (depth * ns)
    pairs = hid // 2
    half = depth
    tile = 2 * depth
    full = own * nr
    signal_peers(("seq", "res"))

    norm_rows(src, xs, xs_inv, own, depth)
    wl_ts = split(wl_t[...])
    left_t = mm3(wl_ts, split(xs[...]), NT)
    low = lax.broadcasted_iota(jnp.int32, (hid, tile), 1) < half
    for u in range(own // 2):
        a = left_t[:, u * tile : (u + 1) * tile]
        b = pltpu.roll(a, half, 1)
        turn[2 * u * hid : (2 * u + 1) * hid, :] = jnp.where(low, a, b)
        turn[(2 * u + 1) * hid : (2 * u + 2) * hid, :] = jnp.where(low, b, a)
    low8 = lax.broadcasted_iota(jnp.int32, (own, tile), 1) < half
    for t in range(pairs):
        even = turn[pl.ds(2 * t, own, stride=hid), :]
        odd = turn[pl.ds(2 * t + 1, own, stride=hid), :]
        left_blk[:, t * tile : (t + 1) * tile] = jnp.where(low8, even, odd)
    for j in range(own):
        cot_blk[:, j * wide : (j + 1) * wide] = cot[pl.ds(j, own, stride=own), :]

    wait_peers(("seq", "res"))
    x_cot = Exchange("seq", lambda t: cot_blk, lambda k: cot_all.at[block(k, own)], s_cot, r_cot)
    x_left = Exchange("res", lambda t: left_blk, lambda k: left_all.at[block(k, own)], s_left, r_left)
    x_cot.start()
    x_left.start()
    cot_all[block(seq_me, own), :] = cot_blk[...]
    left_all[block(res_me, own), :] = left_blk[...]

    norm_rows(tgt, xt, xt_inv, own, depth)
    wr_ts = split(wr_t[...])
    right = mm3(split(xt[...]), wr_ts, NT) * scale
    right_h, right_l = split(right)
    right_k = jnp.concatenate([right_h, right_h, right_l], axis=1)
    rt_h, rt_l = split(right.T)
    rt_hl = jnp.concatenate([rt_h, rt_l], axis=0)
    fh, fl = split(fin[...])
    fin_h[...] = fh
    fin_l[...] = fl

    def make_b(hp, _):
        def stacked(p):
            rows = block(2 * hp + p, hid)
            return jnp.concatenate([fin_h[rows, :], fin_l[rows, :], fin_h[rows, :]], axis=0)

        val = mm(right_k, jnp.concatenate([stacked(0), stacked(1)], axis=1))
        for p in range(2):
            for j in range(own):
                v = val[j * depth : (j + 1) * depth, p * wide : (p + 1) * wide]
                vh, vl = split(v)
                b_h[block(2 * hp + p, depth), j * wide : (j + 1) * wide] = vh
                b_l[block(2 * hp + p, depth), j * wide : (j + 1) * wide] = vl
        return 0

    lax.fori_loop(0, pairs, make_b, 0)

    x_cot.wait_recv()
    ch, cl = split(cot_all[...])
    cot_h[...] = ch
    cot_l[...] = cl

    def make_gls(n, _):
        rows = block(n, 2 * tile)
        gls_part[:, block(n, 2 * tile)] = mm3(
            (cot_h[...], cot_l[...]), (b_h[rows, :], b_l[rows, :]), NT
        )
        return 0

    lax.fori_loop(0, hid * depth // (2 * tile), make_gls, 0)
    x_gls = Exchange("res", lambda t: gls_part.at[block(t, own)], lambda k: gls_in.at[k], s_gls, r_gls)
    x_gls.start()
    gls_in[res_me] = gls_part[block(res_me, own), :]

    x_left.wait_recv()
    lh, ll = split(left_all[...])
    left_h[...] = lh
    left_l[...] = ll
    for t in range(pairs):
        th, tl = split(left_all[:, t * tile : (t + 1) * tile].T)
        lt_h[t * tile : (t + 1) * tile, :] = th
        lt_l[t * tile : (t + 1) * tile, :] = tl
    acc64[...] = jnp.zeros_like(acc64)
    acc32[...] = jnp.zeros_like(acc32)

    def make_db(hp, _):
        a_h = lt_h[block(hp, tile), :]
        a_l = lt_l[block(hp, tile), :]
        a_hl = jnp.concatenate([a_h, a_l], axis=1)
        for jj in range(own // 2):
            cols = slice(2 * jj * wide, 2 * (jj + 1) * wide)
            c_h = cot_h[:, cols]
            val = mm(a_hl, jnp.concatenate([c_h, c_h], axis=0)) + mm(a_h, cot_l[:, cols])
            for q in range(2):
                for p in range(2):
                    v = val[p * depth : (p + 1) * depth, q * wide : (q + 1) * wide]
                    vh, vl = split(v)
                    rows = slice((2 * jj + q) * depth, (2 * jj + q + 1) * depth)
                    db_h[rows, p * wide : (p + 1) * wide] = vh
                    db_l[rows, p * wide : (p + 1) * wide] = vl
        dh = db_h[...]
        dl = db_l[...]
        y = mm(rt_hl, dh)
        grad = y[:hid, :] + y[hid:, :] + mm(rt_h, dl)
        quad = hp // 2
        lanes = pl.ds(pl.multiple_of((hp % 2) * 2 * wide, 2 * wide), 2 * wide)
        big[:, quad, :, lanes] = grad.reshape(hid, 1, 2 * wide)

        def flat(ref):
            return jnp.concatenate(
                [ref[block(2 * hp, hid), :], ref[block(2 * hp + 1, hid), :]], axis=1
            )

        f_h = flat(fin_h)
        acc64[...] += mm(dh, jnp.concatenate([f_h, flat(fin_l)], axis=0), NT)
        acc32[...] += mm(dl, f_h, NT)
        return 0

    lax.fori_loop(0, pairs, make_db, 0)
    per = hid // nr
    x_big = Exchange("res", lambda t: big.at[pl.ds(t * per, per)], lambda k: big_in.at[k], s_big, r_big)
    x_big.start()
    big_in[res_me] = big[pl.ds(res_me * per, per)]

    def make_edge(n, _):
        cols = block(n, 2 * wide)
        edge_part[:, cols] = mm3((left_h[...], left_l[...]), (b_h[:, cols], b_l[:, cols]))
        return 0

    lax.fori_loop(0, own * wide // (2 * wide), make_edge, 0)
    x_edge = Exchange("seq", lambda t: edge_part.at[block(t, own)], lambda k: edge_in.at[k], s_edge, r_edge)
    x_edge.start()
    edge_in[seq_me] = edge_part[block(seq_me, own), :]

    both = acc64[...]
    grs = (both[:, :hid] + both[:, hid:] + acc32[...]) * scale
    xts = split(xt[...])
    up[...] = mm3(split(grs), wr_ts)
    norm_back(up, xt, xt_inv, cols_out, own, depth)
    gr_t = mm3(split(grs.T), xts)
    gb = jnp.sum(cot[...], axis=0, keepdims=True)
    for h in range(2):
        small[:, 2 + h, :, :] = gr_t[:, h * wide : (h + 1) * wide].reshape(hid, 1, wide)
    small[:, 4, :, :] = jnp.broadcast_to(gb, (hid, wide)).reshape(hid, 1, wide)
    for h in range(5, 8):
        small[:, h, :, :] = jnp.zeros((hid, 1, wide), F32)

    x_gls.wait_recv()
    gls = gls_in[0]
    for k in range(1, nr):
        gls = gls + gls_in[k]
    for t in range(pairs):
        v = gls[:, t * tile : (t + 1) * tile]
        turn[pl.ds(2 * t, own, stride=hid), :] = v
        turn[pl.ds(2 * t + 1, own, stride=hid), :] = pltpu.roll(v, half, 1)
    parts = []
    for u in range(own // 2):
        a = turn[2 * u * hid : (2 * u + 1) * hid, :]
        b = turn[(2 * u + 1) * hid : (2 * u + 2) * hid, :]
        parts.append(jnp.where(low, a, pltpu.roll(b, half, 1)))
    gls_t = jnp.concatenate(parts, axis=1)
    gl_t = mm3(split(gls_t), split(xs[...]))
    for h in range(2):
        small[:, h, :, :] = gl_t[:, h * wide : (h + 1) * wide].reshape(hid, 1, wide)
    x_small = Exchange("res", lambda t: small.at[pl.ds(t * per, per)], lambda k: small_in.at[k], s_small, r_small)
    x_small.start()
    small_in[res_me] = small[pl.ds(res_me * per, per)]
    up[...] = mm3(split(gls_t.T), wl_ts)
    norm_back(up, xs, xs_inv, rows_out, own, depth)

    x_big.wait_recv()
    x_small.wait_recv()
    acc1[:, :, :, : 4 * wide] = jnp.sum(big_in[...], axis=0)
    acc1[:, :, :, 4 * wide :] = jnp.sum(small_in[...], axis=0)
    few, quads = seq_chunk(per, ns)
    groups = 8 // quads

    def at(ref, t):
        return ref.at[pl.ds((t // groups) * few, few), pl.ds((t % groups) * quads, quads)]

    x_p2 = Exchange("seq", lambda t: at(acc1, t), lambda k: in2.at[k], s_p2, r_p2)
    x_p2.start()
    in2[seq_me] = at(acc1, seq_me)[...]
    x_p2.wait_recv()
    acc2[...] = jnp.sum(in2[...], axis=0)
    x_p3 = Exchange("seq", lambda t: acc2, lambda k: at(seqs, k), s_p3, r_p3)
    x_p3.start()
    at(seqs, seq_me)[...] = acc2[...]
    x_p3.wait_recv()
    x_p4 = Exchange("res", lambda t: seqs, lambda k: red.at[pl.ds(k * per, per)], s_p4, r_p4)
    x_p4.start()
    red[pl.ds(res_me * per, per)] = seqs[...]

    x_edge.wait_recv()
    edge = edge_in[0]
    for k in range(1, ns):
        edge = edge + edge_in[k]
    for j in range(own):
        edge_out[pl.ds(j, own, stride=own), :] = edge[:, j * wide : (j + 1) * wide] + bias[...]

    x_p4.wait_recv()
    for h in range(hid):
        fin_out[h * hid : (h + 1) * hid, :] = red[:, h // 4, :, (h % 4) * wide : (h % 4 + 1) * wide].reshape(hid, wide)
    for h in range(2):
        lanes = slice(h * wide, (h + 1) * wide)
        gl_out[:, lanes] = red[:, h, :, 4 * wide :].reshape(hid, wide)
        gr_out[:, lanes] = red[:, 2 + h, :, 4 * wide :].reshape(hid, wide)
    gb_out[...] = red[0, 4, :, 4 * wide :]
    for x in (x_cot, x_left, x_gls, x_edge, x_big, x_small, x_p2, x_p3, x_p4):
        x.wait_send()


def seq_chunk(per, ns):
    quads = max(1, 8 // ns)
    return per * 8 // (ns * quads), quads


def to_tiles(x):
    depth, own, chan = x.shape
    return x.reshape(depth, own, 2, chan // 2).swapaxes(1, 2).reshape(-1, chan // 2)


def from_tiles(x, depth, own):
    return x.reshape(depth, 2, own, -1).swapaxes(1, 2).reshape(depth, own, -1)


def body(tgt, src, wl, wr, fin, bias, cot):
    ns = lax.axis_size("seq")
    nr = lax.axis_size("res")
    depth, own, chan = src.shape
    hid = wl.shape[1]
    wide = fin.shape[1]
    flat = own * depth
    per = hid // nr
    few, quads = seq_chunk(per, ns)
    v = pltpu.VMEM
    k = hid * depth
    n = own * wide
    operands = (
        to_tiles(src), to_tiles(tgt), wl.T, wr.T, fin,
        bias.reshape(1, wide), cot.reshape(own * own, wide),
    )
    outs = (
        jax.ShapeDtypeStruct((own * own, wide), F32),
        jax.ShapeDtypeStruct((2 * flat, 128), F32),
        jax.ShapeDtypeStruct((2 * flat, 128), F32),
        jax.ShapeDtypeStruct((hid * hid, wide), F32),
        jax.ShapeDtypeStruct((hid, chan), F32),
        jax.ShapeDtypeStruct((hid, chan), F32),
        jax.ShapeDtypeStruct((1, wide), F32),
    )
    scratch = [
        v((flat, chan), F32), v((flat, 1), F32), v((flat, chan), F32), v((flat, 1), F32),
        v((own * hid, 2 * depth), F32), v((own, k), F32), v((nr * own, k), F32),
        v((nr * own, k), BF16), v((nr * own, k), BF16), v((k, nr * own), BF16), v((k, nr * own), BF16),
        v((own, n), F32), v((ns * own, n), F32), v((ns * own, n), BF16), v((ns * own, n), BF16),
        v((hid * hid, wide), BF16), v((hid * hid, wide), BF16), v((k, n), BF16), v((k, n), BF16),
        v((nr * own, k), F32), v((nr, own, k), F32), v((ns * own, n), F32), v((ns, own, n), F32),
        v((flat, 2 * wide), BF16), v((flat, 2 * wide), BF16), v((flat, 2 * hid), F32), v((flat, hid), F32),
        v((flat, hid), F32), v((flat, chan), F32),
        v((hid, 8, 1, 4 * wide), F32), v((nr, per, 8, 1, 4 * wide), F32),
        v((hid, 8, 1, wide), F32), v((nr, per, 8, 1, wide), F32),
        v((per, 8, 1, 5 * wide), F32), v((ns, few, quads, 1, 5 * wide), F32), v((few, quads, 1, 5 * wide), F32),
        v((per, 8, 1, 5 * wide), F32), v((hid, 8, 1, 5 * wide), F32),
    ]
    for axis in (ns, ns, nr, nr, nr, nr, ns, ns, nr, nr, nr, nr, ns, ns, ns, ns, nr, nr):
        scratch.append(pltpu.SemaphoreType.DMA((axis,)))
    spec = pl.BlockSpec(memory_space=pltpu.MemorySpace.VMEM)
    edge, cols, rows, g_fin, g_wl, g_wr, g_bias = pl.pallas_call(
        functools.partial(kernel, own=own, depth=depth, hid=hid, wide=wide),
        out_shape=outs,
        in_specs=[spec] * len(operands),
        out_specs=(spec,) * len(outs),
        scratch_shapes=scratch,
        compiler_params=pltpu.CompilerParams(
            collective_id=0, has_side_effects=True, vmem_limit_bytes=60 * 2**20
        ),
        name="outer_mean",
    )(*operands)
    return (
        edge.reshape(own, own, wide),
        from_tiles(cols, depth, own),
        from_tiles(rows, depth, own),
        g_wl.T,
        g_wr.T,
        g_fin,
        g_bias.reshape(wide),
    )


def solution(mesh):
    parts = P("seq", "res", None)
    in_specs = (parts, parts, P(), P(), P(), P(), parts)
    out_specs = (parts, parts, parts, P(), P(), P(), P())
    return jax.shard_map(body, mesh=mesh, in_specs=in_specs, out_specs=out_specs, check_vma=False)
```

```python
import functools

import jax
import jax.numpy as jnp
from jax import lax
from jax.experimental import pallas as pl
from jax.experimental.pallas import tpu as pltpu
from jax.sharding import PartitionSpec as P

EPS = 1e-05
RES = (2, 4, 2)
SEMS = 192
F32 = jnp.float32
BF16 = jnp.bfloat16
MESH = pl.DeviceIdType.MESH
NN = (((1,), (0,)), ((), ()))
NT = (((1,), (1,)), ((), ()))


def mm(a, b, dims=NN):
    return lax.dot_general(a, b, dims, preferred_element_type=F32)


def split(x):
    high = x.astype(BF16)
    return high, (x - high.astype(F32)).astype(BF16)


def mm3(a, b, dims=NN):
    return mm(a[0], b[0], dims) + (mm(a[0], b[1], dims) + mm(a[1], b[0], dims))


class Group:
    def __init__(self, size, me, id_of):
        self.size = size
        self.me = me
        self.id_of = id_of

    def each(self, act):
        def one(step, _):
            act(lax.rem(self.me + step, self.size))
            return 0

        if self.size > 1:
            lax.fori_loop(1, self.size, one, 0)


class Semaphores:
    def __init__(self, send, recv):
        self.send = send
        self.recv = recv
        self.used = 0

    def take(self, count):
        self.used += count
        return self.used - count


class Exchange:
    def __init__(self, group, sems, src_of, dst_of):
        self.group = group
        self.sems = sems
        self.base = sems.take(group.size)
        self.src_of = src_of
        self.dst_of = dst_of

    def copy(self, target, slot):
        return pltpu.make_async_remote_copy(
            src_ref=self.src_of(target),
            dst_ref=self.dst_of(slot),
            send_sem=self.sems.send.at[self.base + target],
            recv_sem=self.sems.recv.at[self.base + slot],
            device_id=self.group.id_of(target),
            device_id_type=MESH,
        )

    def start_to(self, peer):
        self.copy(peer, self.group.me).start()

    def wait_from(self, peer):
        self.copy(peer, peer).wait_recv()

    def start(self):
        self.group.each(self.start_to)

    def wait_recv(self):
        self.group.each(self.wait_from)

    def wait_send(self):
        self.group.each(lambda peer: self.copy(peer, self.group.me).wait_send())


def signal_peers(groups):
    barrier = pltpu.get_barrier_semaphore()
    for group in groups:

        def signal(peer, group=group):
            pl.semaphore_signal(
                barrier, inc=1, device_id=group.id_of(peer), device_id_type=MESH
            )

        group.each(signal)


def wait_peers(groups):
    total = sum(group.size - 1 for group in groups)
    pl.semaphore_wait(pltpu.get_barrier_semaphore(), total)


def block(index, rows):
    return pl.ds(pl.multiple_of(index * rows, rows), rows)


def norm_rows(x_ref, normed, inverse, own, depth):
    def one(i, _):
        x = jnp.concatenate(
            [x_ref[pl.ds(i + p * own, depth, stride=2 * own), :] for p in range(2)], axis=1
        )
        centred = x - jnp.mean(x, axis=-1, keepdims=True)
        inv = lax.rsqrt(jnp.mean(centred * centred, axis=-1, keepdims=True) + EPS)
        normed[block(i, depth), :] = centred * inv
        inverse[block(i, depth), :] = inv
        return 0

    lax.fori_loop(0, own, one, 0)


def norm_back(upstream, normed, inverse, out_ref, own, depth):
    for i in range(own):
        rows = slice(i * depth, (i + 1) * depth)
        u = upstream[rows, :]
        y = normed[rows, :]
        first = jnp.mean(u, axis=-1, keepdims=True)
        second = jnp.mean(u * y, axis=-1, keepdims=True)
        g = inverse[rows, :] * (u - first - y * second)
        for p in range(2):
            lanes = slice(p * 128, (p + 1) * 128)
            out_ref[pl.ds(i + p * own, depth, stride=2 * own), :] = g[:, lanes]


def kernel(
    src, tgt, wl_t, wr_t, fin, bias, cot,
    edge_out, cols_out, rows_out, fin_out, gl_out, gr_out, gb_out,
    xs, xs_inv, xt, xt_inv, turn, left_blk, left_all, left_h, left_l, lt_h, lt_l,
    cot_blk, cot_all, cot_h, cot_l, fin_h, fin_l, b_h, b_l,
    gls_part, gls_c, gls_1, gls_x, gls_2, gls_y,
    edge_part, edge_in, db_h, db_l, acc64, acc32, grs_ref, up,
    big, big_c, big_1, big_x, small, small_c, small_1, small_x,
    acc1, in2, acc2, seqs, red, send_sem, recv_sem,
    *, own, depth, hid, wide,
):
    nr = lax.axis_size("res")
    ns = lax.axis_size("seq")
    res_me = lax.axis_index("res")
    seq_me = lax.axis_index("seq")
    scale = 1.0 / (depth * ns)
    pairs = hid // 2
    half = depth
    tile = 2 * depth
    full = own * nr
    yn, xn, cn = RES
    core = lax.rem(res_me, cn)
    ex = lax.rem(res_me // cn, xn)
    wy = res_me // (cn * xn)
    others = [lax.rem(wy + d, yn) for d in range(1, yn)]

    def res_id(y, x, c):
        return (y * xn + x) * cn + c

    g_core = Group(cn, core, lambda m: {"res": res_id(wy, ex, m)})
    g_x = Group(xn, ex, lambda m: {"res": res_id(wy, m, core)})
    g_y = Group(yn, wy, lambda m: {"res": res_id(m, ex, core)})
    g_seq = Group(ns, seq_me, lambda m: {"seq": m})
    g_far = Group(
        yn * ns, wy * ns + seq_me, lambda m: {"res": res_id(m // ns, ex, core), "seq": lax.rem(m, ns)}
    )
    greeted = (g_core, g_x, g_far)
    sems = Semaphores(send_sem, recv_sem)
    signal_peers(greeted)

    norm_rows(src, xs, xs_inv, own, depth)
    wl_ts = split(wl_t[...])
    left_t = mm3(wl_ts, split(xs[...]), NT)
    low = lax.broadcasted_iota(jnp.int32, (hid, tile), 1) < half
    for u in range(own // 2):
        a = left_t[:, u * tile : (u + 1) * tile]
        b = pltpu.roll(a, half, 1)
        turn[2 * u * hid : (2 * u + 1) * hid, :] = jnp.where(low, a, b)
        turn[(2 * u + 1) * hid : (2 * u + 2) * hid, :] = jnp.where(low, b, a)
    low8 = lax.broadcasted_iota(jnp.int32, (own, tile), 1) < half
    for t in range(pairs):
        even = turn[pl.ds(2 * t, own, stride=hid), :]
        odd = turn[pl.ds(2 * t + 1, own, stride=hid), :]
        left_blk[:, t * tile : (t + 1) * tile] = jnp.where(low8, even, odd)
    for j in range(own):
        cot_blk[:, j * wide : (j + 1) * wide] = cot[pl.ds(j, own, stride=own), :]

    wait_peers(greeted)

    def left_at(y, x, c):
        return left_all.at[block(res_id(y, x, c), own)]

    x_cot = Exchange(g_seq, sems, lambda t: cot_blk, lambda k: cot_all.at[block(k, own)])
    left_xs = Exchange(g_x, sems, lambda t: left_blk, lambda k: left_at(wy, k, core))
    left_ys = Exchange(g_y, sems, lambda t: left_blk, lambda k: left_at(k, ex, core))
    left_far = [
        Exchange(g_x, sems, lambda t, y=y: left_at(y, ex, core), lambda k, y=y: left_at(y, k, core))
        for y in others
    ]
    left_own = Exchange(g_core, sems, lambda t: left_blk, lambda k: left_at(wy, ex, k))

    def to_core(y, x):
        return Exchange(
            g_core, sems, lambda t: left_at(y, x, core), lambda k: left_at(y, x, k)
        )

    left_mates = [to_core(y, ex) for y in others]
    steps = [lax.rem(ex + d, xn) for d in range(1, xn)]
    left_mates_x = [to_core(wy, x) for x in steps]
    left_mates_far = [[to_core(y, x) for x in steps] for y in others]
    left_ys.start()
    left_xs.start()
    left_own.start()
    x_cot.start()
    cot_all[block(seq_me, own), :] = cot_blk[...]
    left_all[block(res_me, own), :] = left_blk[...]

    norm_rows(tgt, xt, xt_inv, own, depth)
    left_ys.wait_recv()
    for far, mate in zip(left_far, left_mates):
        far.start()
        mate.start()
    wr_ts = split(wr_t[...])
    right = mm3(split(xt[...]), wr_ts, NT) * scale
    right_h, right_l = split(right)
    right_k = jnp.concatenate([right_h, right_h, right_l], axis=1)
    rt_h, rt_l = split(right.T)
    rt_hl = jnp.concatenate([rt_h, rt_l], axis=0)
    fh, fl = split(fin[...])
    fin_h[...] = fh
    fin_l[...] = fl

    def make_b(hp, _):
        def stacked(p):
            rows = block(2 * hp + p, hid)
            return jnp.concatenate([fin_h[rows, :], fin_l[rows, :], fin_h[rows, :]], axis=0)

        val = mm(right_k, jnp.concatenate([stacked(0), stacked(1)], axis=1))
        for p in range(2):
            for j in range(own):
                v = val[j * depth : (j + 1) * depth, p * wide : (p + 1) * wide]
                vh, vl = split(v)
                b_h[block(2 * hp + p, depth), j * wide : (j + 1) * wide] = vh
                b_l[block(2 * hp + p, depth), j * wide : (j + 1) * wide] = vl
        return 0

    lax.fori_loop(0, pairs, make_b, 0)

    x_cot.wait_recv()
    ch, cl = split(cot_all[...])
    cot_h[...] = ch
    cot_l[...] = cl

    def make_gls(n, _):
        rows = block(n, 2 * tile)
        gls_part[:, block(n, 2 * tile)] = mm3(
            (cot_h[...], cot_l[...]), (b_h[rows, :], b_l[rows, :]), NT
        )
        return 0

    lax.fori_loop(0, hid * depth // (2 * tile), make_gls, 0)
    def gls_at(y, x, c):
        return gls_part.at[block(res_id(y, x, c), own)]

    mate_gls = {}
    for y in range(yn):
        for x in range(xn):
            mate_gls[y, x] = Exchange(
                g_core,
                sems,
                lambda t, y=y, x=x: gls_at(y, x, t),
                lambda k, y=y, x=x: gls_c.at[y * xn + x],
            )
            mate_gls[y, x].start()
    for x, mate in zip(steps, left_mates_x):
        left_xs.wait_from(x)
        mate.start()
    for far, mates in zip(left_far, left_mates_far):
        for x, mate in zip(steps, mates):
            far.wait_from(x)
            mate.start()

    x_gls = [
        Exchange(
            g_x, sems, lambda t, y=y: gls_1.at[y * xn + t], lambda k, y=y: gls_x.at[y * xn + k]
        )
        for y in [wy, *others]
    ]
    for (y, x), mate in mate_gls.items():
        mate.wait_recv()
        at = y * xn + x
        if cn > 1:
            gls_1[at] = gls_at(y, x, core)[...] + gls_c[at]
        else:
            gls_1[at] = gls_at(y, x, core)[...]
    for sent in reversed(x_gls):
        sent.start()

    for mate in [left_own, *left_mates, *left_mates_x, *sum(left_mates_far, [])]:
        mate.wait_recv()
    lh, ll = split(left_all[...])
    left_h[...] = lh
    left_l[...] = ll
    for t in range(pairs):
        th, tl = split(left_all[:, t * tile : (t + 1) * tile].T)
        lt_h[t * tile : (t + 1) * tile, :] = th
        lt_l[t * tile : (t + 1) * tile, :] = tl
    acc64[...] = jnp.zeros_like(acc64)
    acc32[...] = jnp.zeros_like(acc32)

    def make_db(hp, _):
        a_h = lt_h[block(hp, tile), :]
        a_l = lt_l[block(hp, tile), :]
        a_hl = jnp.concatenate([a_h, a_l], axis=1)
        for jj in range(own // 2):
            cols = slice(2 * jj * wide, 2 * (jj + 1) * wide)
            c_h = cot_h[:, cols]
            val = mm(a_hl, jnp.concatenate([c_h, c_h], axis=0)) + mm(a_h, cot_l[:, cols])
            for q in range(2):
                for p in range(2):
                    v = val[p * depth : (p + 1) * depth, q * wide : (q + 1) * wide]
                    vh, vl = split(v)
                    rows = slice((2 * jj + q) * depth, (2 * jj + q + 1) * depth)
                    db_h[rows, p * wide : (p + 1) * wide] = vh
                    db_l[rows, p * wide : (p + 1) * wide] = vl
        dh = db_h[...]
        dl = db_l[...]
        y = mm(rt_hl, dh)
        grad = y[:hid, :] + y[hid:, :] + mm(rt_h, dl)
        quad = hp // 2
        lanes = pl.ds(pl.multiple_of((hp % 2) * 2 * wide, 2 * wide), 2 * wide)
        big[:, quad, :, lanes] = grad.reshape(hid, 1, 2 * wide)

        def flat(ref):
            return jnp.concatenate(
                [ref[block(2 * hp, hid), :], ref[block(2 * hp + 1, hid), :]], axis=1
            )

        f_h = flat(fin_h)
        acc64[...] += mm(dh, jnp.concatenate([f_h, flat(fin_l)], axis=0), NT)
        acc32[...] += mm(dl, f_h, NT)
        return 0

    lax.fori_loop(0, pairs, make_db, 0)
    per_c = hid // cn
    per = per_c // xn

    def start_core(whole, mine):
        out = Exchange(g_core, sems, lambda t: whole.at[pl.ds(t * per_c, per_c)], lambda k: mine)
        out.start()
        return out

    def fold_core(exchange, whole, other, total):
        exchange.wait_recv()
        if cn > 1:
            total[...] = whole[pl.ds(core * per_c, per_c)] + other[...]
        else:
            total[...] = whole[...]

    def start_x(total, arrived):
        out = Exchange(g_x, sems, lambda t: total.at[pl.ds(t * per, per)], lambda k: arrived.at[k])
        out.start()
        arrived[ex] = total[pl.ds(ex * per, per)]
        return out

    core_big = start_core(big, big_c)

    def make_edge(n, _):
        cols = block(n, 2 * wide)
        edge_part[:, cols] = mm3((left_h[...], left_l[...]), (b_h[:, cols], b_l[:, cols]))
        return 0

    lax.fori_loop(0, own * wide // (2 * wide), make_edge, 0)
    fold_core(core_big, big, big_c, big_1)
    x_big = start_x(big_1, big_x)
    x_edge = Exchange(
        g_seq, sems, lambda t: edge_part.at[block(t, own)], lambda k: edge_in.at[k]
    )
    x_edge.start()
    edge_in[seq_me] = edge_part[block(seq_me, own), :]

    both = acc64[...]
    grs = (both[:, :hid] + both[:, hid:] + acc32[...]) * scale
    xts = split(xt[...])
    up[...] = mm3(split(grs), wr_ts)
    norm_back(up, xt, xt_inv, cols_out, own, depth)
    gr_t = mm3(split(grs.T), xts)
    gb = jnp.sum(cot[...], axis=0, keepdims=True)
    for h in range(2):
        small[:, 2 + h, :, :] = gr_t[:, h * wide : (h + 1) * wide].reshape(hid, 1, wide)
    small[:, 4, :, :] = jnp.broadcast_to(gb, (hid, wide)).reshape(hid, 1, wide)
    for h in range(5, 8):
        small[:, h, :, :] = jnp.zeros((hid, 1, wide), F32)

    def fold_x(y, arriving):
        arriving.wait_recv()
        total = gls_1[y * xn + ex]
        for x in steps:
            total = total + gls_x[y * xn + x]
        return total

    y_gls = Exchange(g_y, sems, lambda t: gls_2.at[t], lambda k: gls_y.at[k])
    for y, arriving in zip(others, x_gls[1:]):
        gls_2[y] = fold_x(y, arriving)
        y_gls.start_to(y)
    gls = fold_x(wy, x_gls[0])
    for y in others:
        y_gls.wait_from(y)
        gls = gls + gls_y[y]
    for t in range(pairs):
        v = gls[:, t * tile : (t + 1) * tile]
        turn[pl.ds(2 * t, own, stride=hid), :] = v
        turn[pl.ds(2 * t + 1, own, stride=hid), :] = pltpu.roll(v, half, 1)
    parts = []
    for u in range(own // 2):
        a = turn[2 * u * hid : (2 * u + 1) * hid, :]
        b = turn[(2 * u + 1) * hid : (2 * u + 2) * hid, :]
        parts.append(jnp.where(low, a, pltpu.roll(b, half, 1)))
    gls_t = jnp.concatenate(parts, axis=1)
    gl_t = mm3(split(gls_t), split(xs[...]))
    for h in range(2):
        small[:, h, :, :] = gl_t[:, h * wide : (h + 1) * wide].reshape(hid, 1, wide)
    core_small = start_core(small, small_c)
    up[...] = mm3(split(gls_t.T), wl_ts)
    norm_back(up, xs, xs_inv, rows_out, own, depth)

    fold_core(core_small, small, small_c, small_1)
    x_small = start_x(small_1, small_x)
    x_big.wait_recv()
    x_small.wait_recv()
    acc1[:, :, :, : 4 * wide] = jnp.sum(big_x[...], axis=0)
    acc1[:, :, :, 4 * wide :] = jnp.sum(small_x[...], axis=0)
    few, quads = far_chunk(per, g_far.size)
    groups = 8 // quads

    def at(ref, t):
        return ref.at[pl.ds((t // groups) * few, few), pl.ds(lax.rem(t, groups) * quads, quads)]

    x_p2 = Exchange(g_far, sems, lambda t: at(acc1, t), lambda k: in2.at[k])
    x_p2.start()
    in2[g_far.me] = at(acc1, g_far.me)[...]
    x_p2.wait_recv()
    acc2[...] = jnp.sum(in2[...], axis=0)
    x_p3 = Exchange(g_far, sems, lambda t: acc2, lambda k: at(seqs, k))
    x_p3.start()
    at(seqs, g_far.me)[...] = acc2[...]
    x_p3.wait_recv()

    def red_at(c, x):
        return red.at[pl.ds(c * per_c + x * per, per)]

    x_p4 = Exchange(g_x, sems, lambda t: seqs, lambda k: red_at(core, k))
    x_p4.start()
    mate_own = Exchange(g_core, sems, lambda t: seqs, lambda k: red_at(k, ex))
    mate_own.start()
    red_at(core, ex)[...] = seqs[...]
    mates_red = []
    for x in steps:
        x_p4.wait_from(x)
        mates_red.append(
            Exchange(g_core, sems, lambda t, x=x: red_at(core, x), lambda k, x=x: red_at(k, x))
        )
        mates_red[-1].start()

    x_edge.wait_recv()
    edge = edge_in[0]
    for k in range(1, ns):
        edge = edge + edge_in[k]
    for j in range(own):
        edge_out[pl.ds(j, own, stride=own), :] = edge[:, j * wide : (j + 1) * wide] + bias[...]

    mate_own.wait_recv()
    for mate in mates_red:
        mate.wait_recv()
    for h in range(hid):
        fin_out[h * hid : (h + 1) * hid, :] = red[:, h // 4, :, (h % 4) * wide : (h % 4 + 1) * wide].reshape(hid, wide)
    for h in range(2):
        lanes = slice(h * wide, (h + 1) * wide)
        gl_out[:, lanes] = red[:, h, :, 4 * wide :].reshape(hid, wide)
        gr_out[:, lanes] = red[:, 2 + h, :, 4 * wide :].reshape(hid, wide)
    gb_out[...] = red[0, 4, :, 4 * wide :]
    for sent in (
        x_cot, left_xs, left_ys, left_own, *left_far, *left_mates, *left_mates_x,
        *sum(left_mates_far, []), *mate_gls.values(), *x_gls, y_gls, x_edge, core_big,
        core_small, x_big, x_small, x_p2, x_p3, x_p4, mate_own, *mates_red,
    ):
        sent.wait_send()


def far_chunk(per, members):
    quads = max(1, 8 // members)
    return per * 8 // (members * quads), quads


def to_tiles(x):
    depth, own, chan = x.shape
    return x.reshape(depth, own, 2, chan // 2).swapaxes(1, 2).reshape(-1, chan // 2)


def from_tiles(x, depth, own):
    return x.reshape(depth, 2, own, -1).swapaxes(1, 2).reshape(depth, own, -1)


def body(tgt, src, wl, wr, fin, bias, cot):
    ns = lax.axis_size("seq")
    nr = lax.axis_size("res")
    depth, own, chan = src.shape
    hid = wl.shape[1]
    wide = fin.shape[1]
    flat = own * depth
    yn, xn, cn = RES
    per_c = hid // cn
    per = per_c // xn
    far = yn * ns
    few, quads = far_chunk(per, far)
    v = pltpu.VMEM
    k = hid * depth
    n = own * wide
    operands = (
        to_tiles(src), to_tiles(tgt), wl.T, wr.T, fin,
        bias.reshape(1, wide), cot.reshape(own * own, wide),
    )
    outs = (
        jax.ShapeDtypeStruct((own * own, wide), F32),
        jax.ShapeDtypeStruct((2 * flat, 128), F32),
        jax.ShapeDtypeStruct((2 * flat, 128), F32),
        jax.ShapeDtypeStruct((hid * hid, wide), F32),
        jax.ShapeDtypeStruct((hid, chan), F32),
        jax.ShapeDtypeStruct((hid, chan), F32),
        jax.ShapeDtypeStruct((1, wide), F32),
    )
    scratch = [
        v((flat, chan), F32), v((flat, 1), F32), v((flat, chan), F32), v((flat, 1), F32),
        v((own * hid, 2 * depth), F32), v((own, k), F32), v((nr * own, k), F32),
        v((nr * own, k), BF16), v((nr * own, k), BF16), v((k, nr * own), BF16), v((k, nr * own), BF16),
        v((own, n), F32), v((ns * own, n), F32), v((ns * own, n), BF16), v((ns * own, n), BF16),
        v((hid * hid, wide), BF16), v((hid * hid, wide), BF16), v((k, n), BF16), v((k, n), BF16),
        v((nr * own, k), F32), v((yn * xn, own, k), F32), v((yn * xn, own, k), F32),
        v((yn * xn, own, k), F32), v((yn, own, k), F32), v((yn, own, k), F32),
        v((ns * own, n), F32), v((ns, own, n), F32),
        v((flat, 2 * wide), BF16), v((flat, 2 * wide), BF16), v((flat, 2 * hid), F32), v((flat, hid), F32),
        v((flat, hid), F32), v((flat, chan), F32),
        v((hid, 8, 1, 4 * wide), F32), v((per_c, 8, 1, 4 * wide), F32),
        v((per_c, 8, 1, 4 * wide), F32), v((xn, per, 8, 1, 4 * wide), F32),
        v((hid, 8, 1, wide), F32), v((per_c, 8, 1, wide), F32),
        v((per_c, 8, 1, wide), F32), v((xn, per, 8, 1, wide), F32),
        v((per, 8, 1, 5 * wide), F32), v((far, few, quads, 1, 5 * wide), F32),
        v((few, quads, 1, 5 * wide), F32),
        v((per, 8, 1, 5 * wide), F32), v((hid, 8, 1, 5 * wide), F32),
        pltpu.SemaphoreType.DMA((SEMS,)), pltpu.SemaphoreType.DMA((SEMS,)),
    ]
    spec = pl.BlockSpec(memory_space=pltpu.MemorySpace.VMEM)
    edge, cols, rows, g_fin, g_wl, g_wr, g_bias = pl.pallas_call(
        functools.partial(kernel, own=own, depth=depth, hid=hid, wide=wide),
        out_shape=outs,
        in_specs=[spec] * len(operands),
        out_specs=(spec,) * len(outs),
        scratch_shapes=scratch,
        compiler_params=pltpu.CompilerParams(
            collective_id=0, has_side_effects=True, vmem_limit_bytes=60 * 2**20
        ),
        name="outer_mean",
    )(*operands)
    return (
        edge.reshape(own, own, wide),
        from_tiles(cols, depth, own),
        from_tiles(rows, depth, own),
        g_wl.T,
        g_wr.T,
        g_fin,
        g_bias.reshape(wide),
    )


def solution(mesh):
    parts = P("seq", "res", None)
    in_specs = (parts, parts, P(), P(), P(), P(), parts)
    out_specs = (parts, parts, parts, P(), P(), P(), P())
    return jax.shard_map(body, mesh=mesh, in_specs=in_specs, out_specs=out_specs, check_vma=False)
```

```python
import functools

import jax
import jax.numpy as jnp
from jax import lax
from jax.experimental import pallas as pl
from jax.experimental.pallas import tpu as pltpu
from jax.sharding import PartitionSpec as P

EPS = 1e-05
RES = (2, 4, 2)
SEMS = 72
F32 = jnp.float32
BF16 = jnp.bfloat16
MESH = pl.DeviceIdType.MESH
NN = (((1,), (0,)), ((), ()))
NT = (((1,), (1,)), ((), ()))


def mm(a, b, dims=NN):
    return lax.dot_general(a, b, dims, preferred_element_type=F32)


def split(x):
    high = x.astype(BF16)
    return high, (x - high.astype(F32)).astype(BF16)


def mm3(a, b, dims=NN):
    rows = a[0].shape[0]
    both = mm(jnp.concatenate(a, axis=0), b[0], dims)
    return both[:rows] + (both[rows:] + mm(a[0], b[1], dims))


class Group:
    def __init__(self, size, me, id_of):
        self.size = size
        self.me = me
        self.id_of = id_of

    def each(self, act):
        def one(step, _):
            act(lax.rem(self.me + step, self.size))
            return 0

        if self.size > 1:
            lax.fori_loop(1, self.size, one, 0)


class Semaphores:
    def __init__(self, ref):
        self.ref = ref
        self.used = 0

    def take(self, count=1):
        self.used += count
        return self.used - count


class Exchange:
    def __init__(self, group, sems, src_of, dst_of, bulk=None, single=False, share=None):
        self.group = group
        self.sems = sems
        self.src_of = src_of
        self.dst_of = dst_of
        self.bulk = bulk
        self.single = single
        if share is None:
            self.sent = sems.take()
            self.came = sems.take(group.size if single else 1)
        else:
            self.sent = share.sent
            self.came = sems.take(group.size) if single else share.came

    def describe(self, src, dst, slot, peer):
        return pltpu.make_async_remote_copy(
            src_ref=src,
            dst_ref=dst,
            send_sem=self.sems.ref.at[self.sent],
            recv_sem=self.sems.ref.at[self.came + slot if self.single else self.came],
            device_id=self.group.id_of(peer),
            device_id_type=MESH,
        )

    def start_to(self, peer):
        me = self.group.me
        self.describe(self.src_of(peer), self.dst_of(me), me, peer).start()

    def start(self):
        self.group.each(self.start_to)

    def wait_from(self, peer):
        self.describe(self.src_of(peer), self.dst_of(peer), peer, peer).wait_recv()

    def wait_recv(self):
        if self.group.size > 1:
            self.describe(self.bulk, self.bulk, 0, self.group.me).wait_recv()

    def wait_send(self):
        if self.group.size > 1:
            self.describe(self.bulk, self.bulk, 0, self.group.me).wait_send()


def signal_peers(groups):
    barrier = pltpu.get_barrier_semaphore()
    for group in groups:

        def signal(peer, group=group):
            pl.semaphore_signal(
                barrier, inc=1, device_id=group.id_of(peer), device_id_type=MESH
            )

        group.each(signal)


def wait_peers(groups):
    total = sum(group.size - 1 for group in groups)
    pl.semaphore_wait(pltpu.get_barrier_semaphore(), total)


def block(index, rows):
    return pl.ds(pl.multiple_of(index * rows, rows), rows)


def norm_rows(x_ref, normed, inverse, own, depth):
    def one(i, _):
        x = jnp.concatenate(
            [x_ref[pl.ds(i + p * own, depth, stride=2 * own), :] for p in range(2)], axis=1
        )
        centred = x - jnp.mean(x, axis=-1, keepdims=True)
        inv = lax.rsqrt(jnp.mean(centred * centred, axis=-1, keepdims=True) + EPS)
        normed[block(i, depth), :] = centred * inv
        inverse[block(i, depth), :] = inv
        return 0

    lax.fori_loop(0, own, one, 0)


def norm_back(upstream, normed, inverse, out_ref, own, depth):
    for i in range(own):
        rows = slice(i * depth, (i + 1) * depth)
        u = upstream[rows, :]
        y = normed[rows, :]
        first = jnp.mean(u, axis=-1, keepdims=True)
        second = jnp.mean(u * y, axis=-1, keepdims=True)
        g = inverse[rows, :] * (u - first - y * second)
        for p in range(2):
            lanes = slice(p * 128, (p + 1) * 128)
            out_ref[pl.ds(i + p * own, depth, stride=2 * own), :] = g[:, lanes]


def kernel(
    src_in, tgt_in, wl_in, wr_in, fin_in, bias_in, cot_in,
    edge_res, cols_res, rows_res, fin_res, gl_res, gr_res, gb_res,
    src, tgt, wl_t, wr_t, fin, bias, cot,
    edge_out, cols_out, rows_out, fin_out, gl_out, gr_out, gb_out,
    xs, xs_inv, xt, xt_inv, turn, left_blk, left_all, left_hl, lt_h, lt_l,
    cot_blk, cot_all, cot_hl, cot_t, fin_h, fin_l, b_h, b_l,
    gls_part, gls_c, gls_1, gls_x, gls_2, gls_y,
    edge_part, edge_in, da_h, da_l, db_h, db_l, acc64, acc32, grs_ref, up,
    big, big_c, big_1, big_x, small, small_c, small_1, small_x,
    big_2, big_far, big_3, big_s, big_r, small_2, small_far, small_3, small_s, small_r,
    in_sem, out_sem, comm_sem,
    *, own, depth, hid, wide,
):
    nr = lax.axis_size("res")
    ns = lax.axis_size("seq")
    res_me = lax.axis_index("res")
    seq_me = lax.axis_index("seq")
    scale = 1.0 / (depth * ns)
    pairs = hid // 2
    half = depth
    tile = 2 * depth
    full = own * nr
    yn, xn, cn = RES
    core = lax.rem(res_me, cn)
    ex = lax.rem(res_me // cn, xn)
    wy = res_me // (cn * xn)
    others = [lax.rem(wy + d, yn) for d in range(1, yn)]
    near = sorted(range(1, xn), key=lambda d: min(d, xn - d))
    steps = [lax.rem(ex + d, xn) for d in near]

    def res_id(y, x, c):
        return (y * xn + x) * cn + c

    g_core = Group(cn, core, lambda m: {"res": res_id(wy, ex, m)})
    g_x = Group(xn, ex, lambda m: {"res": res_id(wy, m, core)})
    g_y = Group(yn, wy, lambda m: {"res": res_id(m, ex, core)})
    g_seq = Group(ns, seq_me, lambda m: {"seq": m})
    g_far = Group(
        yn * ns, wy * ns + seq_me, lambda m: {"res": res_id(m // ns, ex, core), "seq": lax.rem(m, ns)}
    )
    greeted = (g_core, g_x, g_far)
    sems = Semaphores(comm_sem)
    loads = [
        pltpu.make_async_copy(a, b, in_sem.at[n])
        for n, (a, b) in enumerate(
            zip(
                (src_in, wl_in, cot_in, tgt_in, wr_in, fin_in, bias_in),
                (src, wl_t, cot, tgt, wr_t, fin, bias),
            )
        )
    ]
    for load in loads:
        load.start()
    signal_peers(greeted)
    for load in loads[:3]:
        load.wait()

    norm_rows(src, xs, xs_inv, own, depth)
    wl_ts = split(wl_t[...])
    left_t = mm3(wl_ts, split(xs[...]), NT)
    low = lax.broadcasted_iota(jnp.int32, (hid, tile), 1) < half
    for u in range(own // 2):
        a = left_t[:, u * tile : (u + 1) * tile]
        b = pltpu.roll(a, half, 1)
        turn[2 * u * hid : (2 * u + 1) * hid, :] = jnp.where(low, a, b)
        turn[(2 * u + 1) * hid : (2 * u + 2) * hid, :] = jnp.where(low, b, a)
    low8 = lax.broadcasted_iota(jnp.int32, (own, tile), 1) < half
    for t in range(pairs):
        even = turn[pl.ds(2 * t, own, stride=hid), :]
        odd = turn[pl.ds(2 * t + 1, own, stride=hid), :]
        left_blk[:, t * tile : (t + 1) * tile] = jnp.where(low8, even, odd)
    for j in range(own):
        cot_blk[:, j * wide : (j + 1) * wide] = cot[pl.ds(j, own, stride=own), :]

    wait_peers(greeted)

    def left_at(y, x, c):
        return left_all.at[block(res_id(y, x, c), own)]

    x_cot = Exchange(
        g_seq, sems, lambda t: cot_blk, lambda k: cot_all.at[block(k, own)],
        cot_all.at[: (ns - 1) * own],
    )
    left_xs = Exchange(
        g_x, sems, lambda t: left_blk, lambda k: left_at(wy, k, core),
        left_all.at[: (xn - 1) * own], single=True,
    )
    left_ys = Exchange(
        g_y, sems, lambda t: left_blk, lambda k: left_at(k, ex, core),
        left_all.at[: (yn - 1) * own],
    )
    left_far = [
        Exchange(
            g_x, sems, lambda t, y=y: left_at(y, ex, core), lambda k, y=y: left_at(y, k, core),
            left_all.at[: (xn - 1) * own], single=True,
        )
        for y in others
    ]
    left_own = Exchange(
        g_core, sems, lambda t: left_blk, lambda k: left_at(wy, ex, k),
        left_all.at[: yn * xn * own],
    )

    def to_core(y, x):
        return Exchange(
            g_core, sems, lambda t: left_at(y, x, core), lambda k: left_at(y, x, k), share=left_own
        )

    left_mates = [to_core(y, ex) for y in others]
    left_mates_x = [to_core(wy, x) for x in steps]
    left_mates_far = [[to_core(y, x) for x in steps] for y in others]
    left_ys.start()
    left_xs.start()
    left_own.start()
    x_cot.start()
    cot_all[block(seq_me, own), :] = cot_blk[...]
    left_all[block(res_me, own), :] = left_blk[...]

    for load in loads[3:]:
        load.wait()
    norm_rows(tgt, xt, xt_inv, own, depth)
    wr_ts = split(wr_t[...])
    right = mm3(split(xt[...]), wr_ts, NT) * scale
    right_h, right_l = split(right)
    right_k = jnp.concatenate([right_h, right_h, right_l], axis=1)
    rt_h, rt_l = split(right.T)
    left_ys.wait_recv()
    for far, mate in zip(left_far, left_mates):
        far.start()
        mate.start()
    rt_hl = jnp.concatenate([rt_h, rt_l], axis=0)
    fh, fl = split(fin[...])
    fin_h[...] = fh
    fin_l[...] = fl

    def make_b(hp, _):
        def stacked(p):
            rows = block(2 * hp + p, hid)
            return jnp.concatenate([fin_h[rows, :], fin_l[rows, :], fin_h[rows, :]], axis=0)

        weights = jnp.concatenate([stacked(0), stacked(1)], axis=1)
        for j in range(own):
            val = mm(right_k[j * depth : (j + 1) * depth], weights)
            vh, vl = split(val)
            for p in range(2):
                rows = block(2 * hp + p, depth)
                lanes = slice(p * wide, (p + 1) * wide)
                b_h[rows, j * wide : (j + 1) * wide] = vh[:, lanes]
                b_l[rows, j * wide : (j + 1) * wide] = vl[:, lanes]
        return 0

    lax.fori_loop(0, pairs, make_b, 0)
    for x, mate in zip(steps, left_mates_x):
        left_xs.wait_from(x)
        mate.start()
    for far, mates in zip(left_far, left_mates_far):
        for x, mate in zip(steps, mates):
            far.wait_from(x)
            mate.start()

    x_cot.wait_recv()
    ch, cl = split(cot_all[...])
    rows_all = ns * own
    cot_hl[:rows_all, :] = ch
    cot_hl[rows_all:, :] = cl
    cot_h = cot_hl.at[:rows_all]
    cot_l = cot_hl.at[rows_all:]
    for j in range(own):
        rows = slice(j * wide, (j + 1) * wide)
        th, tl = split(cot_all[:, rows].T)
        cot_t[rows, :rows_all] = th
        cot_t[rows, rows_all:] = tl

    def make_gls(n, _):
        rows = block(n, 2 * tile)
        y = mm(b_h[rows, :], cot_t[...])
        val = y[:, :rows_all] + (y[:, rows_all:] + mm(b_l[rows, :], cot_t[:, :rows_all]))
        gls_part[:, block(n, 2 * tile)] = val.T
        return 0

    lax.fori_loop(0, hid * depth // (2 * tile), make_gls, 0)

    def gls_at(y, x, c):
        return gls_part.at[block(res_id(y, x, c), own)]

    ys = [wy, *others]
    xs_of = [ex, *steps]
    order = [(dy, dx) for dx in [*range(xn - 1, 0, -1), 0] for dy in [*range(1, yn), 0]]
    mate_gls = {}
    first_gls = None
    for dy, dx in order:
        mate_gls[dy, dx] = Exchange(
            g_core,
            sems,
            lambda t, y=ys[dy], x=xs_of[dx]: gls_at(y, x, t),
            lambda k, y=ys[dy], x=xs_of[dx]: gls_c.at[y * xn + x],
            gls_c,
            single=True,
            share=first_gls,
        )
        first_gls = first_gls or mate_gls[dy, dx]
        mate_gls[dy, dx].start()
    x_gls = [
        Exchange(
            g_x, sems, lambda t, y=y: gls_1.at[y * xn + t], lambda k, y=y: gls_x.at[y * xn + k],
            gls_x.at[: xn - 1],
        )
        for y in ys
    ]

    def pass_gls(some):
        for dy, dx in some:
            if cn > 1:
                mate_gls[dy, dx].wait_from(cn - 1 - core)
            at = ys[dy] * xn + xs_of[dx]
            mine = gls_at(ys[dy], xs_of[dx], core)[...]
            gls_1[at] = mine + gls_c[at] if cn > 1 else mine
            if dx:
                x_gls[dy].start_to(xs_of[dx])

    left_own.wait_recv()
    for t in range(pairs):
        lanes = slice(t * tile, (t + 1) * tile)
        val = left_all[:, lanes]
        lh, ll = split(val)
        left_hl[:full, lanes] = lh
        left_hl[full:, lanes] = ll
        th, tl = split(val.T)
        lt_h[lanes, :] = th
        lt_l[lanes, :] = tl

    tiles = own // 2
    sendable = yn * (xn - 1)
    shares = [-(-sendable * n // tiles) for n in range(tiles + 1)]
    for n in range(tiles):
        cols = slice(2 * n * wide, 2 * (n + 1) * wide)
        y = mm(left_hl[...], b_h[:, cols])
        edge_part[:, cols] = y[:full] + (y[full:] + mm(left_hl[:full], b_l[:, cols]))
        pass_gls(order[shares[n] : shares[n + 1]])
    x_edge = Exchange(
        g_seq, sems, lambda t: edge_part.at[block(t, own)], lambda k: edge_in.at[k],
        edge_in.at[: ns - 1],
    )
    x_edge.start()
    edge_in[seq_me] = edge_part[block(seq_me, own), :]

    acc64[...] = jnp.zeros_like(acc64)
    acc32[...] = jnp.zeros_like(acc32)

    def make_db(q, dst_h, dst_l):
        a_h = lt_h[block(q, 2 * tile), :]
        a_hl = jnp.concatenate([a_h, lt_l[block(q, 2 * tile), :]], axis=1)
        for jj in range(own // 2):
            cols = slice(2 * jj * wide, 2 * (jj + 1) * wide)
            c_h = cot_h[:, cols]
            val = mm(a_hl, jnp.concatenate([c_h, c_h], axis=0)) + mm(a_h, cot_l[:, cols])
            vh, vl = split(val)
            for r in range(2):
                rows = slice((2 * jj + r) * depth, (2 * jj + r + 1) * depth)
                lanes = slice(r * wide, (r + 1) * wide)
                for p in range(4):
                    part = slice(p * depth, (p + 1) * depth)
                    dst_h[rows, p * wide : (p + 1) * wide] = vh[part, lanes]
                    dst_l[rows, p * wide : (p + 1) * wide] = vl[part, lanes]

    def use_db(q, src_h, src_l):
        dh = src_h[...]
        dl = src_l[...]
        y = mm(rt_hl, dh)
        grad = y[:hid, :] + (y[hid:, :] + mm(rt_h, dl))
        big[:, q, :, :] = grad.reshape(hid, 1, 4 * wide)

        def flat(ref):
            return jnp.concatenate([ref[block(4 * q + p, hid), :] for p in range(4)], axis=1)

        f_h = flat(fin_h)
        acc64[...] += mm(dh, jnp.concatenate([f_h, flat(fin_l)], axis=0), NT)
        acc32[...] += mm(dl, f_h, NT)

    def two_db(t, _):
        make_db(2 * t + 1, db_h, db_l)
        use_db(2 * t, da_h, da_l)
        make_db(2 * t + 2, da_h, da_l)
        use_db(2 * t + 1, db_h, db_l)
        return 0

    quads = hid // 4
    make_db(0, da_h, da_l)
    lax.fori_loop(0, 1, two_db, 0)
    pass_gls(order[sendable:])
    lax.fori_loop(1, quads // 2 - 1, two_db, 0)
    make_db(quads - 1, db_h, db_l)
    use_db(quads - 2, da_h, da_l)
    use_db(quads - 1, db_h, db_l)
    per_c = hid // cn
    per = per_c // xn

    def start_core(whole, mine):
        out = Exchange(g_core, sems, lambda t: whole.at[pl.ds(t * per_c, per_c)], lambda k: mine, mine)
        out.start()
        return out

    def fold_core(exchange, whole, other, total):
        exchange.wait_recv()
        if cn > 1:
            total[...] = whole[pl.ds(core * per_c, per_c)] + other[...]
        else:
            total[...] = whole[...]

    def start_x(total, arrived):
        out = Exchange(
            g_x, sems, lambda t: total.at[pl.ds(t * per, per)], lambda k: arrived.at[k],
            arrived.at[: xn - 1],
        )
        out.start()
        arrived[ex] = total[pl.ds(ex * per, per)]
        return out

    core_big = start_core(big, big_c)

    both = acc64[...]
    grs = (both[:, :hid] + both[:, hid:] + acc32[...]) * scale
    xts = split(xt[...])
    gr_t = mm3(split(grs.T), xts)
    gb = jnp.sum(cot[...], axis=0, keepdims=True)
    for h in range(2):
        small[:, 2 + h, :, :] = gr_t[:, h * wide : (h + 1) * wide].reshape(hid, 1, wide)
    small[:, 4, :, :] = jnp.broadcast_to(gb, (hid, wide)).reshape(hid, 1, wide)
    for h in range(5, 8):
        small[:, h, :, :] = jnp.zeros((hid, 1, wide), F32)

    def fold_x(y, arriving):
        arriving.wait_recv()
        total = gls_1[y * xn + ex]
        for x in steps:
            total = total + gls_x[y * xn + x]
        return total

    y_gls = Exchange(
        g_y, sems, lambda t: gls_2.at[t], lambda k: gls_y.at[k], gls_y.at[: yn - 1]
    )
    for y, arriving in zip(others, x_gls[1:]):
        gls_2[y] = fold_x(y, arriving)
        y_gls.start_to(y)
    gls = fold_x(wy, x_gls[0])
    fold_core(core_big, big, big_c, big_1)
    x_big = start_x(big_1, big_x)
    stores = []

    def store(value, result):
        stores.append(pltpu.make_async_copy(value, result, out_sem.at[len(stores)]))
        stores[-1].start()

    up[...] = mm3(split(grs), wr_ts)
    norm_back(up, xt, xt_inv, cols_out, own, depth)
    store(cols_out, cols_res)
    y_gls.wait_recv()
    for y in others:
        gls = gls + gls_y[y]
    for t in range(pairs):
        v = gls[:, t * tile : (t + 1) * tile]
        turn[pl.ds(2 * t, own, stride=hid), :] = v
        turn[pl.ds(2 * t + 1, own, stride=hid), :] = pltpu.roll(v, half, 1)
    parts = []
    for u in range(own // 2):
        a = turn[2 * u * hid : (2 * u + 1) * hid, :]
        b = turn[(2 * u + 1) * hid : (2 * u + 2) * hid, :]
        parts.append(jnp.where(low, a, pltpu.roll(b, half, 1)))
    gls_t = jnp.concatenate(parts, axis=1)
    gl_t = mm3(split(gls_t), split(xs[...]))
    for h in range(2):
        small[:, h, :, :] = gl_t[:, h * wide : (h + 1) * wide].reshape(hid, 1, wide)
    core_small = start_core(small, small_c)

    span_rows, span = far_chunk(per, g_far.size)
    groups = 8 // span

    def at(ref, t):
        return ref.at[
            pl.ds((t // groups) * span_rows, span_rows), pl.ds(lax.rem(t, groups) * span, span)
        ]

    def start_far(exchange, arrived, total, parts):
        exchange.wait_recv()
        total[...] = jnp.sum(arrived[...], axis=0)
        out = Exchange(
            g_far, sems, lambda t: at(total, t), lambda k: parts.at[k], parts.at[: g_far.size - 1]
        )
        out.start()
        parts[g_far.me] = at(total, g_far.me)[...]
        return out

    def start_back(exchange, parts, mine, whole):
        exchange.wait_recv()
        mine[...] = jnp.sum(parts[...], axis=0)
        out = Exchange(
            g_far, sems, lambda t: mine, lambda k: at(whole, k), parts.at[: g_far.size - 1]
        )
        out.start()
        at(whole, g_far.me)[...] = mine[...]
        return out

    def red_at(red, c, x):
        return red.at[pl.ds(c * per_c + x * per, per)]

    def start_wide(exchange, whole, red):
        exchange.wait_recv()
        out = Exchange(
            g_x, sems, lambda t: whole, lambda k: red_at(red, core, k),
            red.at[: (xn - 1) * per], single=True,
        )
        out.start()
        mate = Exchange(
            g_core, sems, lambda t: whole, lambda k: red_at(red, k, ex), red.at[: xn * per]
        )
        mate.start()
        red_at(red, core, ex)[...] = whole[...]
        return out, mate

    def start_mates(wide_pair, red):
        out, mate = wide_pair
        for x in steps:
            out.wait_from(x)
            Exchange(
                g_core,
                sems,
                lambda t, x=x: red_at(red, core, x),
                lambda k, x=x: red_at(red, k, x),
                share=mate,
            ).start()

    far_big = start_far(x_big, big_x, big_2, big_far)
    up[...] = mm3(split(gls_t.T), wl_ts)
    norm_back(up, xs, xs_inv, rows_out, own, depth)
    store(rows_out, rows_res)
    fold_core(core_small, small, small_c, small_1)
    x_small = start_x(small_1, small_x)

    x_edge.wait_recv()
    edge = edge_in[0]
    for k in range(1, ns):
        edge = edge + edge_in[k]
    for j in range(own):
        edge_out[pl.ds(j, own, stride=own), :] = edge[:, j * wide : (j + 1) * wide] + bias[...]
    store(edge_out, edge_res)

    back_big = start_back(far_big, big_far, big_3, big_s)
    far_small = start_far(x_small, small_x, small_2, small_far)
    for sent in (
        x_cot, left_xs, left_ys, left_own, *left_far, first_gls, *x_gls, y_gls, x_edge,
        core_big, core_small, x_big, x_small, far_big,
    ):
        sent.wait_send()
    wide_big = start_wide(back_big, big_s, big_r)
    back_small = start_back(far_small, small_far, small_3, small_s)
    start_mates(wide_big, big_r)
    wide_big[1].wait_recv()
    for h in range(hid):
        fin_out[h * hid : (h + 1) * hid, :] = big_r[
            :, h // 4, :, (h % 4) * wide : (h % 4 + 1) * wide
        ].reshape(hid, wide)
    store(fin_out, fin_res)
    wide_small = start_wide(back_small, small_s, small_r)
    start_mates(wide_small, small_r)
    for sent in (far_small, back_big, back_small, *wide_big):
        sent.wait_send()
    wide_small[1].wait_recv()
    for h in range(2):
        lanes = slice(h * wide, (h + 1) * wide)
        gl_out[:, lanes] = small_r[:, h].reshape(hid, wide)
        gr_out[:, lanes] = small_r[:, 2 + h].reshape(hid, wide)
    gb_out[...] = small_r[0, 4]
    store(gl_out, gl_res)
    store(gr_out, gr_res)
    store(gb_out, gb_res)
    for sent in wide_small:
        sent.wait_send()
    for put in stores:
        put.wait()
    assert sems.used <= SEMS, sems.used


def copy_kernel(*refs):
    count = (len(refs) - 2) // 3
    ins, outs, bufs = refs[:count], refs[count : 2 * count], refs[2 * count : 3 * count]
    sem_in, sem_out = refs[-2:]
    gets = [pltpu.make_async_copy(a, b, sem_in.at[n]) for n, (a, b) in enumerate(zip(ins, bufs))]
    puts = [pltpu.make_async_copy(b, o, sem_out.at[n]) for n, (b, o) in enumerate(zip(bufs, outs))]
    for get in gets:
        get.start()
    for get, put in zip(gets, puts):
        get.wait()
        put.start()
    for put in puts:
        put.wait()


def copy_out(arrays):
    anywhere = pl.BlockSpec(memory_space=pl.ANY)
    return pl.pallas_call(
        copy_kernel,
        out_shape=tuple(jax.ShapeDtypeStruct(a.shape, a.dtype) for a in arrays),
        in_specs=[anywhere] * len(arrays),
        out_specs=(anywhere,) * len(arrays),
        scratch_shapes=[pltpu.VMEM(a.shape, a.dtype) for a in arrays]
        + [pltpu.SemaphoreType.DMA((len(arrays),))] * 2,
        name="copy_out",
    )(*arrays)


def far_chunk(per, members):
    quads = max(1, 8 // members)
    return per * 8 // (members * quads), quads


def to_tiles(x):
    depth, own, chan = x.shape
    return x.reshape(depth, own, 2, chan // 2).swapaxes(1, 2).reshape(-1, chan // 2)


def from_tiles(x, depth, own):
    return x.reshape(depth, 2, own, -1).swapaxes(1, 2).reshape(depth, own, -1)


def body(tgt, src, wl, wr, fin, bias, cot):
    ns = lax.axis_size("seq")
    nr = lax.axis_size("res")
    depth, own, chan = src.shape
    hid = wl.shape[1]
    wide = fin.shape[1]
    flat = own * depth
    yn, xn, cn = RES
    per_c = hid // cn
    per = per_c // xn
    far = yn * ns
    few, quads = far_chunk(per, far)
    v = pltpu.VMEM
    k = hid * depth
    n = own * wide
    operands = (
        to_tiles(src), to_tiles(tgt), wl.T, wr.T, fin,
        bias.reshape(1, wide), cot.reshape(own * own, wide),
    )
    outs = (
        jax.ShapeDtypeStruct((own * own, wide), F32),
        jax.ShapeDtypeStruct((2 * flat, 128), F32),
        jax.ShapeDtypeStruct((2 * flat, 128), F32),
        jax.ShapeDtypeStruct((hid * hid, wide), F32),
        jax.ShapeDtypeStruct((hid, chan), F32),
        jax.ShapeDtypeStruct((hid, chan), F32),
        jax.ShapeDtypeStruct((1, wide), F32),
    )
    scratch = [v(a.shape, F32) for a in (*operands, *outs)] + [
        v((flat, chan), F32), v((flat, 1), F32), v((flat, chan), F32), v((flat, 1), F32),
        v((own * hid, 2 * depth), F32), v((own, k), F32), v((nr * own, k), F32),
        v((2 * nr * own, k), BF16), v((k, nr * own), BF16), v((k, nr * own), BF16),
        v((own, n), F32), v((ns * own, n), F32), v((2 * ns * own, n), BF16), v((n, 2 * ns * own), BF16),
        v((hid * hid, wide), BF16), v((hid * hid, wide), BF16), v((k, n), BF16), v((k, n), BF16),
        v((nr * own, k), F32), v((yn * xn, own, k), F32), v((yn * xn, own, k), F32),
        v((yn * xn, own, k), F32), v((yn, own, k), F32), v((yn, own, k), F32),
        v((ns * own, n), F32), v((ns, own, n), F32),
        v((flat, 4 * wide), BF16), v((flat, 4 * wide), BF16), v((flat, 4 * wide), BF16),
        v((flat, 4 * wide), BF16), v((flat, 2 * hid), F32), v((flat, hid), F32),
        v((flat, hid), F32), v((flat, chan), F32),
        v((hid, 8, 1, 4 * wide), F32), v((per_c, 8, 1, 4 * wide), F32),
        v((per_c, 8, 1, 4 * wide), F32), v((xn, per, 8, 1, 4 * wide), F32),
        v((hid, 8, 1, wide), F32), v((per_c, 8, 1, wide), F32),
        v((per_c, 8, 1, wide), F32), v((xn, per, 8, 1, wide), F32),
    ]
    for lanes in (4 * wide, wide):
        scratch += [
            v((per, 8, 1, lanes), F32), v((far, few, quads, 1, lanes), F32),
            v((few, quads, 1, lanes), F32), v((per, 8, 1, lanes), F32),
            v((hid, 8, 1, lanes), F32),
        ]
    scratch += [
        pltpu.SemaphoreType.DMA((len(operands),)), pltpu.SemaphoreType.DMA((len(outs),)),
        pltpu.SemaphoreType.DMA((SEMS,)),
    ]
    spec = pl.BlockSpec(memory_space=pl.ANY)
    results = pl.pallas_call(
        functools.partial(kernel, own=own, depth=depth, hid=hid, wide=wide),
        out_shape=outs,
        in_specs=[spec] * len(operands),
        out_specs=(spec,) * len(outs),
        scratch_shapes=scratch,
        compiler_params=pltpu.CompilerParams(
            collective_id=0, has_side_effects=True, vmem_limit_bytes=60 * 2**20
        ),
        name="outer_mean",
    )(*operands)
    edge, cols, rows, g_fin, g_wl, g_wr, g_bias = copy_out(results)
    return (
        edge.reshape(own, own, wide),
        from_tiles(cols, depth, own),
        from_tiles(rows, depth, own),
        g_wl.T,
        g_wr.T,
        g_fin,
        g_bias.reshape(wide),
    )


def solution(mesh):
    parts = P("seq", "res", None)
    in_specs = (parts, parts, P(), P(), P(), P(), parts)
    out_specs = (parts, parts, parts, P(), P(), P(), P())
    return jax.shard_map(body, mesh=mesh, in_specs=in_specs, out_specs=out_specs, check_vma=False)
```

```python
import functools

import jax
import jax.numpy as jnp
from jax import lax
from jax.experimental import pallas as pl
from jax.experimental.pallas import tpu as pltpu
from jax.sharding import PartitionSpec as P

EPS = 1e-05
RES = (2, 4, 2)
SEMS = 75
F32 = jnp.float32
BF16 = jnp.bfloat16
MESH = pl.DeviceIdType.MESH
NN = (((1,), (0,)), ((), ()))
NT = (((1,), (1,)), ((), ()))


def mm(a, b, dims=NN):
    return lax.dot_general(a, b, dims, preferred_element_type=F32)


def split(x):
    high = x.astype(BF16)
    return high, (x - high.astype(F32)).astype(BF16)


def mm3(a, b, dims=NN):
    rows = a[0].shape[0]
    both = mm(jnp.concatenate(a, axis=0), b[0], dims)
    return both[:rows] + (both[rows:] + mm(a[0], b[1], dims))


class Group:
    def __init__(self, size, me, id_of):
        self.size = size
        self.me = me
        self.id_of = id_of

    def each(self, act):
        def one(step, _):
            act(lax.rem(self.me + step, self.size))
            return 0

        if self.size > 1:
            lax.fori_loop(1, self.size, one, 0)


class Semaphores:
    def __init__(self, ref):
        self.ref = ref
        self.used = 0

    def take(self, count=1):
        self.used += count
        return self.used - count


class Exchange:
    def __init__(self, group, sems, src_of, dst_of, bulk=None, single=False, share=None):
        self.group = group
        self.sems = sems
        self.src_of = src_of
        self.dst_of = dst_of
        self.bulk = bulk
        self.single = single
        if share is None:
            self.sent = sems.take()
            self.came = sems.take(group.size if single else 1)
        else:
            self.sent = share.sent
            self.came = sems.take(group.size) if single else share.came

    def describe(self, src, dst, slot, peer):
        return pltpu.make_async_remote_copy(
            src_ref=src,
            dst_ref=dst,
            send_sem=self.sems.ref.at[self.sent],
            recv_sem=self.sems.ref.at[self.came + slot if self.single else self.came],
            device_id=self.group.id_of(peer),
            device_id_type=MESH,
        )

    def start_to(self, peer):
        me = self.group.me
        self.describe(self.src_of(peer), self.dst_of(me), me, peer).start()

    def start(self):
        self.group.each(self.start_to)

    def wait_from(self, peer):
        self.describe(self.src_of(peer), self.dst_of(peer), peer, peer).wait_recv()

    def wait_recv(self):
        if self.group.size > 1:
            self.describe(self.bulk, self.bulk, 0, self.group.me).wait_recv()

    def wait_send(self):
        if self.group.size > 1:
            self.describe(self.bulk, self.bulk, 0, self.group.me).wait_send()


def signal_peers(groups):
    barrier = pltpu.get_barrier_semaphore()
    for group in groups:

        def signal(peer, group=group):
            pl.semaphore_signal(
                barrier, inc=1, device_id=group.id_of(peer), device_id_type=MESH
            )

        group.each(signal)


def wait_peers(groups):
    total = sum(group.size - 1 for group in groups)
    pl.semaphore_wait(pltpu.get_barrier_semaphore(), total)


def block(index, rows):
    return pl.ds(pl.multiple_of(index * rows, rows), rows)


def norm_rows(x_ref, normed, inverse, own, depth):
    def one(i, _):
        x = jnp.concatenate(
            [x_ref[pl.ds(i + p * own, depth, stride=2 * own), :] for p in range(2)], axis=1
        )
        centred = x - jnp.mean(x, axis=-1, keepdims=True)
        inv = lax.rsqrt(jnp.mean(centred * centred, axis=-1, keepdims=True) + EPS)
        normed[block(i, depth), :] = centred * inv
        inverse[block(i, depth), :] = inv
        return 0

    lax.fori_loop(0, own, one, 0)


def norm_back(upstream, normed, inverse, out_ref, own, depth):
    for i in range(own):
        rows = slice(i * depth, (i + 1) * depth)
        u = upstream[rows, :]
        y = normed[rows, :]
        first = jnp.mean(u, axis=-1, keepdims=True)
        second = jnp.mean(u * y, axis=-1, keepdims=True)
        g = inverse[rows, :] * (u - first - y * second)
        for p in range(2):
            lanes = slice(p * 128, (p + 1) * 128)
            out_ref[pl.ds(i + p * own, depth, stride=2 * own), :] = g[:, lanes]


def kernel(
    src_in, tgt_in, wl_in, wr_in, fin_in, bias_in, cot_in,
    edge_res, cols_res, rows_res, fin_res, gl_res, gr_res, gb_res,
    src, tgt, wl_t, wr_t, fin, bias, cot,
    edge_out, cols_out, rows_out, fin_out, gl_out, gr_out, gb_out,
    xs, xs_inv, xt, xt_inv, turn, left_blk, left_all, left_hl, lt_h, lt_l,
    cot_blk, cot_all, cot_hl, cot_t, fin_h, fin_l, b_h, b_l,
    gls_part, gls_c, gls_1, gls_x, gls_2, gls_y,
    edge_part, edge_in, da_h, da_l, db_h, db_l, acc64, acc32, grs_ref, up,
    big, big_c, big_1, big_x, small, small_c, small_1, small_x,
    big_2, big_far, big_3, big_s, big_r, small_2, small_far, small_3, small_s, small_r,
    in_sem, out_sem, comm_sem,
    *, own, depth, hid, wide,
):
    nr = lax.axis_size("res")
    ns = lax.axis_size("seq")
    res_me = lax.axis_index("res")
    seq_me = lax.axis_index("seq")
    scale = 1.0 / (depth * ns)
    pairs = hid // 2
    half = depth
    tile = 2 * depth
    full = own * nr
    yn, xn, cn = RES
    core = lax.rem(res_me, cn)
    ex = lax.rem(res_me // cn, xn)
    wy = res_me // (cn * xn)
    others = [lax.rem(wy + d, yn) for d in range(1, yn)]
    near = sorted(range(1, xn), key=lambda d: min(d, xn - d))
    steps = [lax.rem(ex + d, xn) for d in near]

    def res_id(y, x, c):
        return (y * xn + x) * cn + c

    g_core = Group(cn, core, lambda m: {"res": res_id(wy, ex, m)})
    g_x = Group(xn, ex, lambda m: {"res": res_id(wy, m, core)})
    g_y = Group(yn, wy, lambda m: {"res": res_id(m, ex, core)})
    g_seq = Group(ns, seq_me, lambda m: {"seq": m})
    g_far = Group(
        yn * ns, wy * ns + seq_me, lambda m: {"res": res_id(m // ns, ex, core), "seq": lax.rem(m, ns)}
    )
    greeted = (g_core, g_x, g_far)
    sems = Semaphores(comm_sem)
    loads = [
        pltpu.make_async_copy(a, b, in_sem.at[n])
        for n, (a, b) in enumerate(
            zip(
                (src_in, wl_in, cot_in, tgt_in, wr_in, fin_in, bias_in),
                (src, wl_t, cot, tgt, wr_t, fin, bias),
            )
        )
    ]
    for load in loads:
        load.start()
    signal_peers(greeted)
    for load in loads[:3]:
        load.wait()

    norm_rows(src, xs, xs_inv, own, depth)
    wl_ts = split(wl_t[...])
    left_t = mm3(wl_ts, split(xs[...]), NT)
    low = lax.broadcasted_iota(jnp.int32, (hid, tile), 1) < half
    for u in range(own // 2):
        a = left_t[:, u * tile : (u + 1) * tile]
        b = pltpu.roll(a, half, 1)
        turn[2 * u * hid : (2 * u + 1) * hid, :] = jnp.where(low, a, b)
        turn[(2 * u + 1) * hid : (2 * u + 2) * hid, :] = jnp.where(low, b, a)
    low8 = lax.broadcasted_iota(jnp.int32, (own, tile), 1) < half
    for t in range(pairs):
        even = turn[pl.ds(2 * t, own, stride=hid), :]
        odd = turn[pl.ds(2 * t + 1, own, stride=hid), :]
        left_blk[:, t * tile : (t + 1) * tile] = jnp.where(low8, even, odd)
    for j in range(own):
        cot_blk[:, j * wide : (j + 1) * wide] = cot[pl.ds(j, own, stride=own), :]

    wait_peers(greeted)

    def left_at(y, x, c):
        return left_all.at[block(res_id(y, x, c), own)]

    x_cot = Exchange(
        g_seq, sems, lambda t: cot_blk, lambda k: cot_all.at[block(k, own)],
        cot_all.at[: (ns - 1) * own],
    )
    left_xs = Exchange(
        g_x, sems, lambda t: left_blk, lambda k: left_at(wy, k, core),
        left_all.at[: (xn - 1) * own], single=True,
    )
    left_ys = Exchange(
        g_y, sems, lambda t: left_blk, lambda k: left_at(k, ex, core),
        left_all.at[: (yn - 1) * own],
    )
    left_far = [
        Exchange(
            g_x, sems, lambda t, y=y: left_at(y, ex, core), lambda k, y=y: left_at(y, k, core),
            left_all.at[: (xn - 1) * own], single=True,
        )
        for y in others
    ]
    left_own = Exchange(
        g_core, sems, lambda t: left_blk, lambda k: left_at(wy, ex, k),
        left_all.at[: yn * xn * own],
    )

    def to_core(y, x):
        return Exchange(
            g_core, sems, lambda t: left_at(y, x, core), lambda k: left_at(y, x, k), share=left_own
        )

    left_mates = [to_core(y, ex) for y in others]
    left_mates_x = [to_core(wy, x) for x in steps]
    left_mates_far = [[to_core(y, x) for x in steps] for y in others]
    left_ys.start()
    left_xs.start()
    left_own.start()
    x_cot.start()
    cot_all[block(seq_me, own), :] = cot_blk[...]
    left_all[block(res_me, own), :] = left_blk[...]

    for load in loads[3:]:
        load.wait()
    norm_rows(tgt, xt, xt_inv, own, depth)
    wr_ts = split(wr_t[...])
    right = mm3(split(xt[...]), wr_ts, NT) * scale
    right_h, right_l = split(right)
    right_k = jnp.concatenate([right_h, right_h, right_l], axis=1)
    rt_h, rt_l = split(right.T)
    left_ys.wait_recv()
    for far, mate in zip(left_far, left_mates):
        far.start()
        mate.start()
    rt_hl = jnp.concatenate([rt_h, rt_l], axis=0)
    fh, fl = split(fin[...])
    fin_h[...] = fh
    fin_l[...] = fl

    def make_b(hp, _):
        def stacked(p):
            rows = block(2 * hp + p, hid)
            return jnp.concatenate([fin_h[rows, :], fin_l[rows, :], fin_h[rows, :]], axis=0)

        weights = jnp.concatenate([stacked(0), stacked(1)], axis=1)
        for j in range(own):
            val = mm(right_k[j * depth : (j + 1) * depth], weights)
            vh, vl = split(val)
            for p in range(2):
                rows = block(2 * hp + p, depth)
                lanes = slice(p * wide, (p + 1) * wide)
                b_h[rows, j * wide : (j + 1) * wide] = vh[:, lanes]
                b_l[rows, j * wide : (j + 1) * wide] = vl[:, lanes]
        return 0

    lax.fori_loop(0, pairs, make_b, 0)
    for x, mate in zip(steps, left_mates_x):
        left_xs.wait_from(x)
        mate.start()
    for far, mates in zip(left_far, left_mates_far):
        for x, mate in zip(steps, mates):
            far.wait_from(x)
            mate.start()

    x_cot.wait_recv()
    ch, cl = split(cot_all[...])
    rows_all = ns * own
    cot_hl[:rows_all, :] = ch
    cot_hl[rows_all:, :] = cl
    cot_h = cot_hl.at[:rows_all]
    cot_l = cot_hl.at[rows_all:]
    for j in range(own):
        rows = slice(j * wide, (j + 1) * wide)
        th, tl = split(cot_all[:, rows].T)
        cot_t[rows, :rows_all] = th
        cot_t[rows, rows_all:] = tl

    def make_gls(n, _):
        rows = block(n, 8 * tile)
        y = mm(b_h[rows, :], cot_t[...])
        val = y[:, :rows_all] + (y[:, rows_all:] + mm(b_l[rows, :], cot_t[:, :rows_all]))
        gls_part[:, block(n, 8 * tile)] = val.T
        return 0

    lax.fori_loop(0, hid * depth // (8 * tile), make_gls, 0)

    def gls_at(y, x, c):
        return gls_part.at[block(res_id(y, x, c), own)]

    ys = [wy, *others]
    xs_of = [ex, *steps]
    order = [(dy, dx) for dx in [*range(xn - 1, 0, -1), 0] for dy in [*range(1, yn), 0]]
    mate_gls = {}
    first_gls = None
    for dy, dx in order:
        mate_gls[dy, dx] = Exchange(
            g_core,
            sems,
            lambda t, y=ys[dy], x=xs_of[dx]: gls_at(y, x, t),
            lambda k, y=ys[dy], x=xs_of[dx]: gls_c.at[y * xn + x],
            gls_c,
            single=True,
            share=first_gls,
        )
        first_gls = first_gls or mate_gls[dy, dx]
        mate_gls[dy, dx].start()
    x_gls = [
        Exchange(
            g_x, sems, lambda t, y=y: gls_1.at[y * xn + t], lambda k, y=y: gls_x.at[y * xn + k],
            gls_x.at[: xn - 1],
        )
        for y in ys
    ]

    def pass_gls(some):
        for dy, dx in some:
            if cn > 1:
                mate_gls[dy, dx].wait_from(cn - 1 - core)
            at = ys[dy] * xn + xs_of[dx]
            mine = gls_at(ys[dy], xs_of[dx], core)[...]
            gls_1[at] = mine + gls_c[at] if cn > 1 else mine
            if dx:
                x_gls[dy].start_to(xs_of[dx])

    left_own.wait_recv()
    for t in range(pairs):
        lanes = slice(t * tile, (t + 1) * tile)
        val = left_all[:, lanes]
        lh, ll = split(val)
        left_hl[:full, lanes] = lh
        left_hl[full:, lanes] = ll
        th, tl = split(val.T)
        lt_h[lanes, :] = th
        lt_l[lanes, :] = tl

    tiles = own // 2
    for n in range(tiles):
        cols = slice(2 * n * wide, 2 * (n + 1) * wide)
        y = mm(left_hl[...], b_h[:, cols])
        edge_part[:, cols] = y[:full] + (y[full:] + mm(left_hl[:full], b_l[:, cols]))
    x_edge = Exchange(
        g_seq, sems, lambda t: edge_part.at[block(t, own)], lambda k: edge_in.at[k],
        edge_in.at[: ns - 1],
    )
    x_edge.start()
    edge_in[seq_me] = edge_part[block(seq_me, own), :]

    acc64[...] = jnp.zeros_like(acc64)
    acc32[...] = jnp.zeros_like(acc32)

    def make_db(q, dst_h, dst_l):
        a_h = lt_h[block(q, 2 * tile), :]
        a_hl = jnp.concatenate([a_h, lt_l[block(q, 2 * tile), :]], axis=1)
        for jj in range(own // 2):
            cols = slice(2 * jj * wide, 2 * (jj + 1) * wide)
            c_h = cot_h[:, cols]
            val = mm(a_hl, jnp.concatenate([c_h, c_h], axis=0)) + mm(a_h, cot_l[:, cols])
            vh, vl = split(val)
            for r in range(2):
                rows = slice((2 * jj + r) * depth, (2 * jj + r + 1) * depth)
                lanes = slice(r * wide, (r + 1) * wide)
                for p in range(4):
                    part = slice(p * depth, (p + 1) * depth)
                    dst_h[rows, p * wide : (p + 1) * wide] = vh[part, lanes]
                    dst_l[rows, p * wide : (p + 1) * wide] = vl[part, lanes]

    def use_db(q, src_h, src_l):
        dh = src_h[...]
        dl = src_l[...]
        y = mm(rt_hl, dh)
        grad = y[:hid, :] + (y[hid:, :] + mm(rt_h, dl))
        big[:, q, :, :] = grad.reshape(hid, 1, 4 * wide)

        def flat(ref):
            return jnp.concatenate([ref[block(4 * q + p, hid), :] for p in range(4)], axis=1)

        f_h = flat(fin_h)
        acc64[...] += mm(dh, jnp.concatenate([f_h, flat(fin_l)], axis=0), NT)
        acc32[...] += mm(dl, f_h, NT)

    def two_db(t, _):
        make_db(2 * t + 1, db_h, db_l)
        use_db(2 * t, da_h, da_l)
        make_db(2 * t + 2, da_h, da_l)
        use_db(2 * t + 1, db_h, db_l)
        return 0

    per_c = hid // cn
    per = per_c // xn

    def start_core(whole, mine, quads):
        out = Exchange(
            g_core, sems, lambda t: whole.at[pl.ds(t * per_c, per_c), quads],
            lambda k: mine.at[:, quads], mine.at[:, quads],
        )
        out.start()
        return out

    def fold_core(exchange, whole, other, total, quads):
        exchange.wait_recv()
        if cn > 1:
            total[:, quads] = whole[pl.ds(core * per_c, per_c), quads] + other[:, quads]
        else:
            total[:, quads] = whole[:, quads]

    def start_x(total, arrived, quads):
        out = Exchange(
            g_x, sems, lambda t: total.at[pl.ds(t * per, per), quads],
            lambda k: arrived.at[k, :, quads], arrived.at[: xn - 1, :, quads],
        )
        out.start()
        arrived[ex, :, quads] = total[pl.ds(ex * per, per), quads]
        return out

    halves = [pl.ds(0, 4), pl.ds(4, 4)]
    every = pl.ds(0, 8)
    quads = hid // 4
    pass_gls(order[:1])
    make_db(0, da_h, da_l)
    pass_gls(order[1:2])
    for t in range(quads // 2 - 1):
        lax.fori_loop(t, t + 1, two_db, 0)
        pass_gls(order[2 * t + 2 : 2 * t + 4])
        if t == quads // 4 - 1:
            core_big = [start_core(big, big_c, halves[0])]
    make_db(quads - 1, db_h, db_l)
    use_db(quads - 2, da_h, da_l)
    use_db(quads - 1, db_h, db_l)
    core_big.append(start_core(big, big_c, halves[1]))
    fold_core(core_big[0], big, big_c, big_1, halves[0])
    x_big = [start_x(big_1, big_x, halves[0])]

    both = acc64[...]
    grs = (both[:, :hid] + both[:, hid:] + acc32[...]) * scale
    xts = split(xt[...])
    gr_t = mm3(split(grs.T), xts)
    gb = jnp.sum(cot[...], axis=0, keepdims=True)
    for h in range(2):
        small[:, 2 + h, :, :] = gr_t[:, h * wide : (h + 1) * wide].reshape(hid, 1, wide)
    small[:, 4, :, :] = jnp.broadcast_to(gb, (hid, wide)).reshape(hid, 1, wide)
    for h in range(5, 8):
        small[:, h, :, :] = jnp.zeros((hid, 1, wide), F32)

    def fold_x(y, arriving):
        arriving.wait_recv()
        total = gls_1[y * xn + ex]
        for x in steps:
            total = total + gls_x[y * xn + x]
        return total

    y_gls = Exchange(
        g_y, sems, lambda t: gls_2.at[t], lambda k: gls_y.at[k], gls_y.at[: yn - 1]
    )
    for y, arriving in zip(others, x_gls[1:]):
        gls_2[y] = fold_x(y, arriving)
        y_gls.start_to(y)
    gls = fold_x(wy, x_gls[0])
    fold_core(core_big[1], big, big_c, big_1, halves[1])
    x_big.append(start_x(big_1, big_x, halves[1]))
    stores = []

    def store(value, result):
        stores.append(pltpu.make_async_copy(value, result, out_sem.at[len(stores)]))
        stores[-1].start()

    up[...] = mm3(split(grs), wr_ts)
    norm_back(up, xt, xt_inv, cols_out, own, depth)
    store(cols_out, cols_res)
    y_gls.wait_recv()
    for y in others:
        gls = gls + gls_y[y]
    for t in range(pairs):
        v = gls[:, t * tile : (t + 1) * tile]
        turn[pl.ds(2 * t, own, stride=hid), :] = v
        turn[pl.ds(2 * t + 1, own, stride=hid), :] = pltpu.roll(v, half, 1)
    parts = []
    for u in range(own // 2):
        a = turn[2 * u * hid : (2 * u + 1) * hid, :]
        b = turn[(2 * u + 1) * hid : (2 * u + 2) * hid, :]
        parts.append(jnp.where(low, a, pltpu.roll(b, half, 1)))
    gls_t = jnp.concatenate(parts, axis=1)
    gl_t = mm3(split(gls_t), split(xs[...]))
    for h in range(2):
        small[:, h, :, :] = gl_t[:, h * wide : (h + 1) * wide].reshape(hid, 1, wide)
    core_small = start_core(small, small_c, every)

    span_rows, span = far_chunk(per, g_far.size)
    groups = 8 // span

    def at(ref, t):
        return ref.at[
            pl.ds((t // groups) * span_rows, span_rows), pl.ds(lax.rem(t, groups) * span, span)
        ]

    def start_far(exchanges, arrived, total, parts):
        for exchange in exchanges:
            exchange.wait_recv()
        total[...] = jnp.sum(arrived[...], axis=0)
        out = Exchange(
            g_far, sems, lambda t: at(total, t), lambda k: parts.at[k], parts.at[: g_far.size - 1]
        )
        out.start()
        parts[g_far.me] = at(total, g_far.me)[...]
        return out

    def start_back(exchange, parts, mine, whole):
        exchange.wait_recv()
        mine[...] = jnp.sum(parts[...], axis=0)
        out = Exchange(
            g_far, sems, lambda t: mine, lambda k: at(whole, k), parts.at[: g_far.size - 1]
        )
        out.start()
        at(whole, g_far.me)[...] = mine[...]
        return out

    def red_at(red, c, x):
        return red.at[pl.ds(c * per_c + x * per, per)]

    def start_wide(exchange, whole, red):
        exchange.wait_recv()
        out = Exchange(
            g_x, sems, lambda t: whole, lambda k: red_at(red, core, k),
            red.at[: (xn - 1) * per], single=True,
        )
        out.start()
        mate = Exchange(
            g_core, sems, lambda t: whole, lambda k: red_at(red, k, ex), red.at[: xn * per]
        )
        mate.start()
        red_at(red, core, ex)[...] = whole[...]
        return out, mate

    def start_mates(wide_pair, red):
        out, mate = wide_pair
        for x in steps:
            out.wait_from(x)
            Exchange(
                g_core,
                sems,
                lambda t, x=x: red_at(red, core, x),
                lambda k, x=x: red_at(red, k, x),
                share=mate,
            ).start()

    up[...] = mm3(split(gls_t.T), wl_ts)
    norm_back(up, xs, xs_inv, rows_out, own, depth)
    store(rows_out, rows_res)
    fold_core(core_small, small, small_c, small_1, every)
    x_small = start_x(small_1, small_x, every)
    far_big = start_far(x_big, big_x, big_2, big_far)

    x_edge.wait_recv()
    edge = edge_in[0]
    for k in range(1, ns):
        edge = edge + edge_in[k]
    for j in range(own):
        edge_out[pl.ds(j, own, stride=own), :] = edge[:, j * wide : (j + 1) * wide] + bias[...]
    store(edge_out, edge_res)

    far_small = start_far([x_small], small_x, small_2, small_far)
    back_big = start_back(far_big, big_far, big_3, big_s)
    for sent in (
        x_cot, left_xs, left_ys, left_own, *left_far, first_gls, *x_gls, y_gls, x_edge,
        *core_big, core_small, *x_big, x_small, far_big,
    ):
        sent.wait_send()
    back_small = start_back(far_small, small_far, small_3, small_s)
    wide_big = start_wide(back_big, big_s, big_r)
    start_mates(wide_big, big_r)
    wide_small = start_wide(back_small, small_s, small_r)
    wide_big[1].wait_recv()
    for h in range(hid):
        fin_out[h * hid : (h + 1) * hid, :] = big_r[
            :, h // 4, :, (h % 4) * wide : (h % 4 + 1) * wide
        ].reshape(hid, wide)
    store(fin_out, fin_res)
    start_mates(wide_small, small_r)
    for sent in (far_small, back_big, back_small, *wide_big):
        sent.wait_send()
    wide_small[1].wait_recv()
    for h in range(2):
        lanes = slice(h * wide, (h + 1) * wide)
        gl_out[:, lanes] = small_r[:, h].reshape(hid, wide)
        gr_out[:, lanes] = small_r[:, 2 + h].reshape(hid, wide)
    gb_out[...] = small_r[0, 4]
    store(gl_out, gl_res)
    store(gr_out, gr_res)
    store(gb_out, gb_res)
    for sent in wide_small:
        sent.wait_send()
    for put in stores:
        put.wait()
    assert sems.used <= SEMS, sems.used


def copy_kernel(*refs):
    count = (len(refs) - 2) // 3
    ins, outs, bufs = refs[:count], refs[count : 2 * count], refs[2 * count : 3 * count]
    sem_in, sem_out = refs[-2:]
    gets = [pltpu.make_async_copy(a, b, sem_in.at[n]) for n, (a, b) in enumerate(zip(ins, bufs))]
    puts = [pltpu.make_async_copy(b, o, sem_out.at[n]) for n, (b, o) in enumerate(zip(bufs, outs))]
    for get in gets:
        get.start()
    for get, put in zip(gets, puts):
        get.wait()
        put.start()
    for put in puts:
        put.wait()


def copy_out(arrays):
    anywhere = pl.BlockSpec(memory_space=pl.ANY)
    return pl.pallas_call(
        copy_kernel,
        out_shape=tuple(jax.ShapeDtypeStruct(a.shape, a.dtype) for a in arrays),
        in_specs=[anywhere] * len(arrays),
        out_specs=(anywhere,) * len(arrays),
        scratch_shapes=[pltpu.VMEM(a.shape, a.dtype) for a in arrays]
        + [pltpu.SemaphoreType.DMA((len(arrays),))] * 2,
        name="copy_out",
    )(*arrays)


def far_chunk(per, members):
    quads = max(1, 8 // members)
    return per * 8 // (members * quads), quads


def to_tiles(x):
    depth, own, chan = x.shape
    return x.reshape(depth, own, 2, chan // 2).swapaxes(1, 2).reshape(-1, chan // 2)


def from_tiles(x, depth, own):
    return x.reshape(depth, 2, own, -1).swapaxes(1, 2).reshape(depth, own, -1)


def body(tgt, src, wl, wr, fin, bias, cot):
    ns = lax.axis_size("seq")
    nr = lax.axis_size("res")
    depth, own, chan = src.shape
    hid = wl.shape[1]
    wide = fin.shape[1]
    flat = own * depth
    yn, xn, cn = RES
    per_c = hid // cn
    per = per_c // xn
    far = yn * ns
    few, quads = far_chunk(per, far)
    v = pltpu.VMEM
    k = hid * depth
    n = own * wide
    operands = (
        to_tiles(src), to_tiles(tgt), wl.T, wr.T, fin,
        bias.reshape(1, wide), cot.reshape(own * own, wide),
    )
    outs = (
        jax.ShapeDtypeStruct((own * own, wide), F32),
        jax.ShapeDtypeStruct((2 * flat, 128), F32),
        jax.ShapeDtypeStruct((2 * flat, 128), F32),
        jax.ShapeDtypeStruct((hid * hid, wide), F32),
        jax.ShapeDtypeStruct((hid, chan), F32),
        jax.ShapeDtypeStruct((hid, chan), F32),
        jax.ShapeDtypeStruct((1, wide), F32),
    )
    scratch = [v(a.shape, F32) for a in (*operands, *outs)] + [
        v((flat, chan), F32), v((flat, 1), F32), v((flat, chan), F32), v((flat, 1), F32),
        v((own * hid, 2 * depth), F32), v((own, k), F32), v((nr * own, k), F32),
        v((2 * nr * own, k), BF16), v((k, nr * own), BF16), v((k, nr * own), BF16),
        v((own, n), F32), v((ns * own, n), F32), v((2 * ns * own, n), BF16), v((n, 2 * ns * own), BF16),
        v((hid * hid, wide), BF16), v((hid * hid, wide), BF16), v((k, n), BF16), v((k, n), BF16),
        v((nr * own, k), F32), v((yn * xn, own, k), F32), v((yn * xn, own, k), F32),
        v((yn * xn, own, k), F32), v((yn, own, k), F32), v((yn, own, k), F32),
        v((ns * own, n), F32), v((ns, own, n), F32),
        v((flat, 4 * wide), BF16), v((flat, 4 * wide), BF16), v((flat, 4 * wide), BF16),
        v((flat, 4 * wide), BF16), v((flat, 2 * hid), F32), v((flat, hid), F32),
        v((flat, hid), F32), v((flat, chan), F32),
        v((hid, 8, 1, 4 * wide), F32), v((per_c, 8, 1, 4 * wide), F32),
        v((per_c, 8, 1, 4 * wide), F32), v((xn, per, 8, 1, 4 * wide), F32),
        v((hid, 8, 1, wide), F32), v((per_c, 8, 1, wide), F32),
        v((per_c, 8, 1, wide), F32), v((xn, per, 8, 1, wide), F32),
    ]
    for lanes in (4 * wide, wide):
        scratch += [
            v((per, 8, 1, lanes), F32), v((far, few, quads, 1, lanes), F32),
            v((few, quads, 1, lanes), F32), v((per, 8, 1, lanes), F32),
            v((hid, 8, 1, lanes), F32),
        ]
    scratch += [
        pltpu.SemaphoreType.DMA((len(operands),)), pltpu.SemaphoreType.DMA((len(outs),)),
        pltpu.SemaphoreType.DMA((SEMS,)),
    ]
    spec = pl.BlockSpec(memory_space=pl.ANY)
    results = pl.pallas_call(
        functools.partial(kernel, own=own, depth=depth, hid=hid, wide=wide),
        out_shape=outs,
        in_specs=[spec] * len(operands),
        out_specs=(spec,) * len(outs),
        scratch_shapes=scratch,
        compiler_params=pltpu.CompilerParams(
            collective_id=0, has_side_effects=True, vmem_limit_bytes=60 * 2**20
        ),
        name="outer_mean",
    )(*operands)
    edge, cols, rows, g_fin, g_wl, g_wr, g_bias = copy_out(results)
    return (
        edge.reshape(own, own, wide),
        from_tiles(cols, depth, own),
        from_tiles(rows, depth, own),
        g_wl.T,
        g_wr.T,
        g_fin,
        g_bias.reshape(wide),
    )


def solution(mesh):
    parts = P("seq", "res", None)
    in_specs = (parts, parts, P(), P(), P(), P(), parts)
    out_specs = (parts, parts, parts, P(), P(), P(), P())
    return jax.shard_map(body, mesh=mesh, in_specs=in_specs, out_specs=out_specs, check_vma=False)
```

```python
import functools

import jax
import jax.numpy as jnp
from jax import lax
from jax.experimental import pallas as pl
from jax.experimental.pallas import tpu as pltpu
from jax.sharding import PartitionSpec as P

EPS = 1e-05
RES = (2, 4, 2)
SEMS = 75
F32 = jnp.float32
BF16 = jnp.bfloat16
MESH = pl.DeviceIdType.MESH
NN = (((1,), (0,)), ((), ()))
NT = (((1,), (1,)), ((), ()))


def mm(a, b, dims=NN):
    return lax.dot_general(a, b, dims, preferred_element_type=F32)


def split(x):
    high = x.astype(BF16)
    return high, (x - high.astype(F32)).astype(BF16)


def mm3(a, b, dims=NN):
    rows = a[0].shape[0]
    both = mm(jnp.concatenate(a, axis=0), b[0], dims)
    return both[:rows] + (both[rows:] + mm(a[0], b[1], dims))


class Group:
    def __init__(self, size, me, id_of, peer=None):
        self.size = size
        self.me = me
        self.id_of = id_of
        self.plain = lambda n: lax.rem(me + 1 + n, size)
        self.peer = peer or self.plain

    def each(self, act, plain=False):
        def one(n, _):
            act(self.plain(n) if plain else self.peer(n))
            return 0

        if self.size > 1:
            lax.fori_loop(0, self.size - 1, one, 0)


class Semaphores:
    def __init__(self, ref):
        self.ref = ref
        self.used = 0

    def take(self, count=1):
        self.used += count
        return self.used - count


class Exchange:
    def __init__(self, group, sems, src_of, dst_of, bulk=None, single=False, share=None):
        self.group = group
        self.sems = sems
        self.src_of = src_of
        self.dst_of = dst_of
        self.bulk = bulk
        self.single = single
        if share is None:
            self.sent = sems.take()
            self.came = sems.take(group.size if single else 1)
        else:
            self.sent = share.sent
            self.came = sems.take(group.size) if single else share.came

    def describe(self, src, dst, slot, peer):
        return pltpu.make_async_remote_copy(
            src_ref=src,
            dst_ref=dst,
            send_sem=self.sems.ref.at[self.sent],
            recv_sem=self.sems.ref.at[self.came + slot if self.single else self.came],
            device_id=self.group.id_of(peer),
            device_id_type=MESH,
        )

    def start_to(self, peer):
        me = self.group.me
        self.describe(self.src_of(peer), self.dst_of(me), me, peer).start()

    def start(self):
        self.group.each(self.start_to)

    def wait_from(self, peer):
        self.describe(self.src_of(peer), self.dst_of(peer), peer, peer).wait_recv()

    def wait_recv(self):
        if self.group.size > 1:
            self.describe(self.bulk, self.bulk, 0, self.group.me).wait_recv()

    def wait_send(self):
        if self.group.size > 1:
            self.describe(self.bulk, self.bulk, 0, self.group.me).wait_send()


def signal_peers(groups):
    barrier = pltpu.get_barrier_semaphore()
    for group in groups:

        def signal(peer, group=group):
            pl.semaphore_signal(
                barrier, inc=1, device_id=group.id_of(peer), device_id_type=MESH
            )

        group.each(signal, plain=True)


def wait_peers(groups):
    total = sum(group.size - 1 for group in groups)
    pl.semaphore_wait(pltpu.get_barrier_semaphore(), total)


def block(index, rows):
    return pl.ds(pl.multiple_of(index * rows, rows), rows)


def norm_rows(x_ref, normed, inverse, own, depth):
    def one(i, _):
        x = jnp.concatenate(
            [x_ref[pl.ds(i + p * own, depth, stride=2 * own), :] for p in range(2)], axis=1
        )
        centred = x - jnp.mean(x, axis=-1, keepdims=True)
        inv = lax.rsqrt(jnp.mean(centred * centred, axis=-1, keepdims=True) + EPS)
        normed[block(i, depth), :] = centred * inv
        inverse[block(i, depth), :] = inv
        return 0

    lax.fori_loop(0, own, one, 0)


def norm_back(upstream, normed, inverse, out_ref, own, depth):
    for i in range(own):
        rows = slice(i * depth, (i + 1) * depth)
        u = upstream[rows, :]
        y = normed[rows, :]
        first = jnp.mean(u, axis=-1, keepdims=True)
        second = jnp.mean(u * y, axis=-1, keepdims=True)
        g = inverse[rows, :] * (u - first - y * second)
        for p in range(2):
            lanes = slice(p * 128, (p + 1) * 128)
            out_ref[pl.ds(i + p * own, depth, stride=2 * own), :] = g[:, lanes]


def kernel(
    src_in, tgt_in, wl_in, wr_in, fin_in, bias_in, cot_in,
    edge_res, cols_res, rows_res, fin_res, gl_res, gr_res, gb_res,
    src, tgt, wl_t, wr_t, fin, bias, cot,
    edge_out, cols_out, rows_out, fin_out, gl_out, gr_out, gb_out,
    xs, xs_inv, xt, xt_inv, turn, left_blk, left_all, left_hl, lt_h, lt_l,
    cot_blk, cot_all, cot_hl, cot_t, fin_h, fin_l, b_h, b_l,
    gls_part, gls_c, gls_1, gls_x, gls_2, gls_y,
    edge_part, edge_in, da_h, da_l, db_h, db_l, acc64, acc32, grs_ref, up,
    big, big_c, big_1, big_x, small, small_c, small_1, small_x,
    big_2, big_far, big_3, big_s, big_r, small_2, small_far, small_3, small_s, small_r,
    in_sem, out_sem, comm_sem,
    *, own, depth, hid, wide,
):
    nr = lax.axis_size("res")
    ns = lax.axis_size("seq")
    res_me = lax.axis_index("res")
    seq_me = lax.axis_index("seq")
    scale = 1.0 / (depth * ns)
    pairs = hid // 2
    half = depth
    tile = 2 * depth
    full = own * nr
    yn, xn, cn = RES
    core = lax.rem(res_me, cn)
    ex = lax.rem(res_me // cn, xn)
    wy = res_me // (cn * xn)
    others = [lax.rem(wy + d, yn) for d in range(1, yn)]
    near = sorted(range(1, xn), key=lambda d: min(d, xn - d))
    steps = [lax.rem(ex + d, xn) for d in near]

    def res_id(y, x, c):
        return (y * xn + x) * cn + c

    g_core = Group(cn, core, lambda m: {"res": res_id(wy, ex, m)})
    g_x = Group(xn, ex, lambda m: {"res": res_id(wy, m, core)})
    g_y = Group(yn, wy, lambda m: {"res": res_id(m, ex, core)})
    zn = ns // 2
    zed = seq_me // 2

    def seq_peer(k, flip):
        turn_z = (1 - 2 * lax.rem(k, 2)) * ((k + 1) // 2)
        return lax.rem(zed + zn + zn // 2 + turn_z, zn) * 2 + lax.rem(seq_me + flip, 2)

    def far_peer(n):
        rest = lax.rem(n + 1, 2 * yn)
        return lax.rem(wy + rest // 2, yn) * ns + seq_peer(n // (2 * yn), lax.rem(rest, 2))

    g_seq = Group(ns, seq_me, lambda m: {"seq": m})
    g_far = Group(
        yn * ns,
        wy * ns + seq_me,
        lambda m: {"res": res_id(m // ns, ex, core), "seq": lax.rem(m, ns)},
        far_peer,
    )
    greeted = (g_core, g_x, g_far)
    sems = Semaphores(comm_sem)
    loads = [
        pltpu.make_async_copy(a, b, in_sem.at[n])
        for n, (a, b) in enumerate(
            zip(
                (src_in, wl_in, cot_in, tgt_in, wr_in, fin_in, bias_in),
                (src, wl_t, cot, tgt, wr_t, fin, bias),
            )
        )
    ]
    for load in loads:
        load.start()
    signal_peers(greeted)
    for load in loads[:3]:
        load.wait()

    norm_rows(src, xs, xs_inv, own, depth)
    wl_ts = split(wl_t[...])
    left_t = mm3(wl_ts, split(xs[...]), NT)
    low = lax.broadcasted_iota(jnp.int32, (hid, tile), 1) < half
    for u in range(own // 2):
        a = left_t[:, u * tile : (u + 1) * tile]
        b = pltpu.roll(a, half, 1)
        turn[2 * u * hid : (2 * u + 1) * hid, :] = jnp.where(low, a, b)
        turn[(2 * u + 1) * hid : (2 * u + 2) * hid, :] = jnp.where(low, b, a)
    low8 = lax.broadcasted_iota(jnp.int32, (own, tile), 1) < half
    for t in range(pairs):
        even = turn[pl.ds(2 * t, own, stride=hid), :]
        odd = turn[pl.ds(2 * t + 1, own, stride=hid), :]
        left_blk[:, t * tile : (t + 1) * tile] = jnp.where(low8, even, odd)
    for j in range(own):
        cot_blk[:, j * wide : (j + 1) * wide] = cot[pl.ds(j, own, stride=own), :]

    wait_peers(greeted)

    def left_at(y, x, c):
        return left_all.at[block(res_id(y, x, c), own)]

    x_cot = Exchange(
        g_seq, sems, lambda t: cot_blk, lambda k: cot_all.at[block(k, own)],
        cot_all.at[: (ns - 1) * own],
    )
    left_xs = Exchange(
        g_x, sems, lambda t: left_blk, lambda k: left_at(wy, k, core),
        left_all.at[: (xn - 1) * own], single=True,
    )
    left_ys = Exchange(
        g_y, sems, lambda t: left_blk, lambda k: left_at(k, ex, core),
        left_all.at[: (yn - 1) * own],
    )
    left_far = [
        Exchange(
            g_x, sems, lambda t, y=y: left_at(y, ex, core), lambda k, y=y: left_at(y, k, core),
            left_all.at[: (xn - 1) * own], single=True,
        )
        for y in others
    ]
    left_own = Exchange(
        g_core, sems, lambda t: left_blk, lambda k: left_at(wy, ex, k),
        left_all.at[: yn * xn * own],
    )

    def to_core(y, x):
        return Exchange(
            g_core, sems, lambda t: left_at(y, x, core), lambda k: left_at(y, x, k), share=left_own
        )

    left_mates = [to_core(y, ex) for y in others]
    left_mates_x = [to_core(wy, x) for x in steps]
    left_mates_far = [[to_core(y, x) for x in steps] for y in others]
    left_ys.start()
    left_xs.start()
    left_own.start()
    x_cot.start()
    cot_all[block(seq_me, own), :] = cot_blk[...]
    left_all[block(res_me, own), :] = left_blk[...]

    for load in loads[3:]:
        load.wait()
    norm_rows(tgt, xt, xt_inv, own, depth)
    wr_ts = split(wr_t[...])
    right = mm3(split(xt[...]), wr_ts, NT) * scale
    right_h, right_l = split(right)
    right_k = jnp.concatenate([right_h, right_h, right_l], axis=1)
    rt_h, rt_l = split(right.T)
    left_ys.wait_recv()
    for far, mate in zip(left_far, left_mates):
        far.start()
        mate.start()
    rt_hl = jnp.concatenate([rt_h, rt_l], axis=0)
    fh, fl = split(fin[...])
    fin_h[...] = fh
    fin_l[...] = fl

    def make_b(hp, _):
        def stacked(p):
            rows = block(2 * hp + p, hid)
            return jnp.concatenate([fin_h[rows, :], fin_l[rows, :], fin_h[rows, :]], axis=0)

        weights = jnp.concatenate([stacked(0), stacked(1)], axis=1)
        for j in range(own):
            val = mm(right_k[j * depth : (j + 1) * depth], weights)
            vh, vl = split(val)
            for p in range(2):
                rows = block(2 * hp + p, depth)
                lanes = slice(p * wide, (p + 1) * wide)
                b_h[rows, j * wide : (j + 1) * wide] = vh[:, lanes]
                b_l[rows, j * wide : (j + 1) * wide] = vl[:, lanes]
        return 0

    lax.fori_loop(0, pairs, make_b, 0)
    for x, mate in zip(steps, left_mates_x):
        left_xs.wait_from(x)
        mate.start()
    for far, mates in zip(left_far, left_mates_far):
        for x, mate in zip(steps, mates):
            far.wait_from(x)
            mate.start()

    x_cot.wait_recv()
    ch, cl = split(cot_all[...])
    rows_all = ns * own
    cot_hl[:rows_all, :] = ch
    cot_hl[rows_all:, :] = cl
    cot_h = cot_hl.at[:rows_all]
    cot_l = cot_hl.at[rows_all:]
    for j in range(own):
        rows = slice(j * wide, (j + 1) * wide)
        th, tl = split(cot_all[:, rows].T)
        cot_t[rows, :rows_all] = th
        cot_t[rows, rows_all:] = tl

    def make_gls(n, _):
        rows = block(n, 8 * tile)
        y = mm(b_h[rows, :], cot_t[...])
        val = y[:, :rows_all] + (y[:, rows_all:] + mm(b_l[rows, :], cot_t[:, :rows_all]))
        gls_part[:, block(n, 8 * tile)] = val.T
        return 0

    lax.fori_loop(0, hid * depth // (8 * tile), make_gls, 0)

    def gls_at(y, x, c):
        return gls_part.at[block(res_id(y, x, c), own)]

    ys = [wy, *others]
    xs_of = [ex, *steps]
    order = [(dy, dx) for dx in [*range(xn - 1, 0, -1), 0] for dy in [*range(1, yn), 0]]
    mate_gls = {}
    first_gls = None
    for dy, dx in order:
        mate_gls[dy, dx] = Exchange(
            g_core,
            sems,
            lambda t, y=ys[dy], x=xs_of[dx]: gls_at(y, x, t),
            lambda k, y=ys[dy], x=xs_of[dx]: gls_c.at[y * xn + x],
            gls_c,
            single=True,
            share=first_gls,
        )
        first_gls = first_gls or mate_gls[dy, dx]
        mate_gls[dy, dx].start()
    x_gls = [
        Exchange(
            g_x, sems, lambda t, y=y: gls_1.at[y * xn + t], lambda k, y=y: gls_x.at[y * xn + k],
            gls_x.at[: xn - 1],
        )
        for y in ys
    ]

    def pass_gls(some):
        for dy, dx in some:
            if cn > 1:
                mate_gls[dy, dx].wait_from(cn - 1 - core)
            at = ys[dy] * xn + xs_of[dx]
            mine = gls_at(ys[dy], xs_of[dx], core)[...]
            gls_1[at] = mine + gls_c[at] if cn > 1 else mine
            if dx:
                x_gls[dy].start_to(xs_of[dx])

    left_own.wait_recv()
    for t in range(pairs):
        lanes = slice(t * tile, (t + 1) * tile)
        val = left_all[:, lanes]
        lh, ll = split(val)
        left_hl[:full, lanes] = lh
        left_hl[full:, lanes] = ll
        th, tl = split(val.T)
        lt_h[lanes, :] = th
        lt_l[lanes, :] = tl

    tiles = own // 2
    for n in range(tiles):
        cols = slice(2 * n * wide, 2 * (n + 1) * wide)
        y = mm(left_hl[...], b_h[:, cols])
        edge_part[:, cols] = y[:full] + (y[full:] + mm(left_hl[:full], b_l[:, cols]))
    x_edge = Exchange(
        g_seq, sems, lambda t: edge_part.at[block(t, own)], lambda k: edge_in.at[k],
        edge_in.at[: ns - 1],
    )
    x_edge.start()
    edge_in[seq_me] = edge_part[block(seq_me, own), :]

    acc64[...] = jnp.zeros_like(acc64)
    acc32[...] = jnp.zeros_like(acc32)

    def make_db(q, dst_h, dst_l):
        a_h = lt_h[block(q, 2 * tile), :]
        a_hl = jnp.concatenate([a_h, lt_l[block(q, 2 * tile), :]], axis=1)
        for jj in range(own // 2):
            cols = slice(2 * jj * wide, 2 * (jj + 1) * wide)
            c_h = cot_h[:, cols]
            val = mm(a_hl, jnp.concatenate([c_h, c_h], axis=0)) + mm(a_h, cot_l[:, cols])
            vh, vl = split(val)
            for r in range(2):
                rows = slice((2 * jj + r) * depth, (2 * jj + r + 1) * depth)
                lanes = slice(r * wide, (r + 1) * wide)
                for p in range(4):
                    part = slice(p * depth, (p + 1) * depth)
                    dst_h[rows, p * wide : (p + 1) * wide] = vh[part, lanes]
                    dst_l[rows, p * wide : (p + 1) * wide] = vl[part, lanes]

    def use_db(q, src_h, src_l):
        dh = src_h[...]
        dl = src_l[...]
        y = mm(rt_hl, dh)
        grad = y[:hid, :] + (y[hid:, :] + mm(rt_h, dl))
        big[:, q, :, :] = grad.reshape(hid, 1, 4 * wide)

        def flat(ref):
            return jnp.concatenate([ref[block(4 * q + p, hid), :] for p in range(4)], axis=1)

        f_h = flat(fin_h)
        acc64[...] += mm(dh, jnp.concatenate([f_h, flat(fin_l)], axis=0), NT)
        acc32[...] += mm(dl, f_h, NT)

    def two_db(t, _):
        make_db(2 * t + 1, db_h, db_l)
        use_db(2 * t, da_h, da_l)
        make_db(2 * t + 2, da_h, da_l)
        use_db(2 * t + 1, db_h, db_l)
        return 0

    per_c = hid // cn
    per = per_c // xn

    def start_core(whole, mine, quads):
        out = Exchange(
            g_core, sems, lambda t: whole.at[pl.ds(t * per_c, per_c), quads],
            lambda k: mine.at[:, quads], mine.at[:, quads],
        )
        out.start()
        return out

    def fold_core(exchange, whole, other, total, quads):
        exchange.wait_recv()
        if cn > 1:
            total[:, quads] = whole[pl.ds(core * per_c, per_c), quads] + other[:, quads]
        else:
            total[:, quads] = whole[:, quads]

    def start_x(total, arrived, quads):
        out = Exchange(
            g_x, sems, lambda t: total.at[pl.ds(t * per, per), quads],
            lambda k: arrived.at[k, :, quads], arrived.at[: xn - 1, :, quads],
        )
        out.start()
        arrived[ex, :, quads] = total[pl.ds(ex * per, per), quads]
        return out

    halves = [pl.ds(0, 4), pl.ds(4, 4)]
    every = pl.ds(0, 8)
    quads = hid // 4
    pass_gls(order[:1])
    make_db(0, da_h, da_l)
    pass_gls(order[1:2])
    for t in range(quads // 2 - 1):
        lax.fori_loop(t, t + 1, two_db, 0)
        pass_gls(order[2 * t + 2 : 2 * t + 4])
        if t == quads // 4 - 1:
            core_big = [start_core(big, big_c, halves[0])]
    make_db(quads - 1, db_h, db_l)
    use_db(quads - 2, da_h, da_l)
    use_db(quads - 1, db_h, db_l)
    core_big.append(start_core(big, big_c, halves[1]))
    fold_core(core_big[0], big, big_c, big_1, halves[0])
    x_big = [start_x(big_1, big_x, halves[0])]

    both = acc64[...]
    grs = (both[:, :hid] + both[:, hid:] + acc32[...]) * scale
    xts = split(xt[...])
    gr_t = mm3(split(grs.T), xts)
    gb = jnp.sum(cot[...], axis=0, keepdims=True)
    for h in range(2):
        small[:, 2 + h, :, :] = gr_t[:, h * wide : (h + 1) * wide].reshape(hid, 1, wide)
    small[:, 4, :, :] = jnp.broadcast_to(gb, (hid, wide)).reshape(hid, 1, wide)
    for h in range(5, 8):
        small[:, h, :, :] = jnp.zeros((hid, 1, wide), F32)

    def fold_x(y, arriving):
        arriving.wait_recv()
        total = gls_1[y * xn + ex]
        for x in steps:
            total = total + gls_x[y * xn + x]
        return total

    y_gls = Exchange(
        g_y, sems, lambda t: gls_2.at[t], lambda k: gls_y.at[k], gls_y.at[: yn - 1]
    )
    for y, arriving in zip(others, x_gls[1:]):
        gls_2[y] = fold_x(y, arriving)
        y_gls.start_to(y)
    gls = fold_x(wy, x_gls[0])
    fold_core(core_big[1], big, big_c, big_1, halves[1])
    x_big.append(start_x(big_1, big_x, halves[1]))
    stores = []

    def store(value, result):
        stores.append(pltpu.make_async_copy(value, result, out_sem.at[len(stores)]))
        stores[-1].start()

    up[...] = mm3(split(grs), wr_ts)
    norm_back(up, xt, xt_inv, cols_out, own, depth)
    store(cols_out, cols_res)
    y_gls.wait_recv()
    for y in others:
        gls = gls + gls_y[y]
    for t in range(pairs):
        v = gls[:, t * tile : (t + 1) * tile]
        turn[pl.ds(2 * t, own, stride=hid), :] = v
        turn[pl.ds(2 * t + 1, own, stride=hid), :] = pltpu.roll(v, half, 1)
    parts = []
    for u in range(own // 2):
        a = turn[2 * u * hid : (2 * u + 1) * hid, :]
        b = turn[(2 * u + 1) * hid : (2 * u + 2) * hid, :]
        parts.append(jnp.where(low, a, pltpu.roll(b, half, 1)))
    gls_t = jnp.concatenate(parts, axis=1)
    gl_t = mm3(split(gls_t), split(xs[...]))
    for h in range(2):
        small[:, h, :, :] = gl_t[:, h * wide : (h + 1) * wide].reshape(hid, 1, wide)
    core_small = start_core(small, small_c, every)

    span_rows, span = far_chunk(per, g_far.size)
    groups = 8 // span

    def at(ref, t):
        return ref.at[
            pl.ds((t // groups) * span_rows, span_rows), pl.ds(lax.rem(t, groups) * span, span)
        ]

    def start_far(exchanges, arrived, total, parts):
        for exchange in exchanges:
            exchange.wait_recv()
        total[...] = jnp.sum(arrived[...], axis=0)
        out = Exchange(
            g_far, sems, lambda t: at(total, t), lambda k: parts.at[k], parts.at[: g_far.size - 1]
        )
        out.start()
        parts[g_far.me] = at(total, g_far.me)[...]
        return out

    def start_back(exchange, parts, mine, whole):
        exchange.wait_recv()
        mine[...] = jnp.sum(parts[...], axis=0)
        out = Exchange(
            g_far, sems, lambda t: mine, lambda k: at(whole, k), parts.at[: g_far.size - 1]
        )
        out.start()
        at(whole, g_far.me)[...] = mine[...]
        return out

    def red_at(red, c, x):
        return red.at[pl.ds(c * per_c + x * per, per)]

    def start_wide(exchange, whole, red):
        exchange.wait_recv()
        out = Exchange(
            g_x, sems, lambda t: whole, lambda k: red_at(red, core, k),
            red.at[: (xn - 1) * per], single=True,
        )
        out.start()
        mate = Exchange(
            g_core, sems, lambda t: whole, lambda k: red_at(red, k, ex), red.at[: xn * per]
        )
        mate.start()
        red_at(red, core, ex)[...] = whole[...]
        return out, mate

    def start_mates(wide_pair, red):
        out, mate = wide_pair
        for x in steps:
            out.wait_from(x)
            Exchange(
                g_core,
                sems,
                lambda t, x=x: red_at(red, core, x),
                lambda k, x=x: red_at(red, k, x),
                share=mate,
            ).start()

    up[...] = mm3(split(gls_t.T), wl_ts)
    norm_back(up, xs, xs_inv, rows_out, own, depth)
    store(rows_out, rows_res)
    fold_core(core_small, small, small_c, small_1, every)
    x_small = start_x(small_1, small_x, every)
    far_big = start_far(x_big, big_x, big_2, big_far)

    x_edge.wait_recv()
    edge = edge_in[0]
    for k in range(1, ns):
        edge = edge + edge_in[k]
    for j in range(own):
        edge_out[pl.ds(j, own, stride=own), :] = edge[:, j * wide : (j + 1) * wide] + bias[...]
    store(edge_out, edge_res)

    far_small = start_far([x_small], small_x, small_2, small_far)
    back_big = start_back(far_big, big_far, big_3, big_s)
    for sent in (
        x_cot, left_xs, left_ys, left_own, *left_far, first_gls, *x_gls, y_gls, x_edge,
        *core_big, core_small, *x_big, x_small, far_big,
    ):
        sent.wait_send()
    back_small = start_back(far_small, small_far, small_3, small_s)
    wide_big = start_wide(back_big, big_s, big_r)
    start_mates(wide_big, big_r)
    wide_small = start_wide(back_small, small_s, small_r)
    wide_big[1].wait_recv()
    for h in range(hid):
        fin_out[h * hid : (h + 1) * hid, :] = big_r[
            :, h // 4, :, (h % 4) * wide : (h % 4 + 1) * wide
        ].reshape(hid, wide)
    store(fin_out, fin_res)
    start_mates(wide_small, small_r)
    for sent in (far_small, back_big, back_small, *wide_big):
        sent.wait_send()
    wide_small[1].wait_recv()
    for h in range(2):
        lanes = slice(h * wide, (h + 1) * wide)
        gl_out[:, lanes] = small_r[:, h].reshape(hid, wide)
        gr_out[:, lanes] = small_r[:, 2 + h].reshape(hid, wide)
    gb_out[...] = small_r[0, 4]
    store(gl_out, gl_res)
    store(gr_out, gr_res)
    store(gb_out, gb_res)
    for sent in wide_small:
        sent.wait_send()
    for put in stores:
        put.wait()
    assert sems.used <= SEMS, sems.used


def copy_kernel(*refs):
    count = (len(refs) - 1) // 2
    puts = [
        pltpu.make_async_copy(a, b, refs[-1].at[n])
        for n, (a, b) in enumerate(zip(refs[:count], refs[count : 2 * count]))
    ]
    for put in puts:
        put.start()
    for put in puts:
        put.wait()


def copy_out(arrays):
    return pl.pallas_call(
        copy_kernel,
        out_shape=tuple(jax.ShapeDtypeStruct(a.shape, a.dtype) for a in arrays),
        in_specs=[pl.BlockSpec(memory_space=pl.ANY)] * len(arrays),
        out_specs=(pl.BlockSpec(memory_space=pltpu.MemorySpace.HBM),) * len(arrays),
        scratch_shapes=[pltpu.SemaphoreType.DMA((len(arrays),))],
        compiler_params=pltpu.CompilerParams(vmem_limit_bytes=2**20),
        name="copy_out",
    )(*arrays)


def far_chunk(per, members):
    quads = max(1, 8 // members)
    return per * 8 // (members * quads), quads


def to_tiles(x):
    depth, own, chan = x.shape
    return x.reshape(depth, own, 2, chan // 2).swapaxes(1, 2).reshape(-1, chan // 2)


def from_tiles(x, depth, own):
    return x.reshape(depth, 2, own, -1).swapaxes(1, 2).reshape(depth, own, -1)


def body(tgt, src, wl, wr, fin, bias, cot):
    ns = lax.axis_size("seq")
    nr = lax.axis_size("res")
    depth, own, chan = src.shape
    hid = wl.shape[1]
    wide = fin.shape[1]
    flat = own * depth
    yn, xn, cn = RES
    per_c = hid // cn
    per = per_c // xn
    far = yn * ns
    few, quads = far_chunk(per, far)
    v = pltpu.VMEM
    k = hid * depth
    n = own * wide
    operands = (
        to_tiles(src), to_tiles(tgt), wl.T, wr.T, fin,
        bias.reshape(1, wide), cot.reshape(own * own, wide),
    )
    outs = (
        jax.ShapeDtypeStruct((own * own, wide), F32),
        jax.ShapeDtypeStruct((2 * flat, 128), F32),
        jax.ShapeDtypeStruct((2 * flat, 128), F32),
        jax.ShapeDtypeStruct((hid * hid, wide), F32),
        jax.ShapeDtypeStruct((hid, chan), F32),
        jax.ShapeDtypeStruct((hid, chan), F32),
        jax.ShapeDtypeStruct((1, wide), F32),
    )
    scratch = [v(a.shape, F32) for a in (*operands, *outs)] + [
        v((flat, chan), F32), v((flat, 1), F32), v((flat, chan), F32), v((flat, 1), F32),
        v((own * hid, 2 * depth), F32), v((own, k), F32), v((nr * own, k), F32),
        v((2 * nr * own, k), BF16), v((k, nr * own), BF16), v((k, nr * own), BF16),
        v((own, n), F32), v((ns * own, n), F32), v((2 * ns * own, n), BF16), v((n, 2 * ns * own), BF16),
        v((hid * hid, wide), BF16), v((hid * hid, wide), BF16), v((k, n), BF16), v((k, n), BF16),
        v((nr * own, k), F32), v((yn * xn, own, k), F32), v((yn * xn, own, k), F32),
        v((yn * xn, own, k), F32), v((yn, own, k), F32), v((yn, own, k), F32),
        v((ns * own, n), F32), v((ns, own, n), F32),
        v((flat, 4 * wide), BF16), v((flat, 4 * wide), BF16), v((flat, 4 * wide), BF16),
        v((flat, 4 * wide), BF16), v((flat, 2 * hid), F32), v((flat, hid), F32),
        v((flat, hid), F32), v((flat, chan), F32),
        v((hid, 8, 1, 4 * wide), F32), v((per_c, 8, 1, 4 * wide), F32),
        v((per_c, 8, 1, 4 * wide), F32), v((xn, per, 8, 1, 4 * wide), F32),
        v((hid, 8, 1, wide), F32), v((per_c, 8, 1, wide), F32),
        v((per_c, 8, 1, wide), F32), v((xn, per, 8, 1, wide), F32),
    ]
    for lanes in (4 * wide, wide):
        scratch += [
            v((per, 8, 1, lanes), F32), v((far, few, quads, 1, lanes), F32),
            v((few, quads, 1, lanes), F32), v((per, 8, 1, lanes), F32),
            v((hid, 8, 1, lanes), F32),
        ]
    scratch += [
        pltpu.SemaphoreType.DMA((len(operands),)), pltpu.SemaphoreType.DMA((len(outs),)),
        pltpu.SemaphoreType.DMA((SEMS,)),
    ]
    spec = pl.BlockSpec(memory_space=pl.ANY)
    operands = tuple(pltpu.with_memory_space_constraint(a, pltpu.MemorySpace.HBM) for a in operands)
    results = pl.pallas_call(
        functools.partial(kernel, own=own, depth=depth, hid=hid, wide=wide),
        out_shape=outs,
        in_specs=[pl.BlockSpec(memory_space=pltpu.MemorySpace.HBM)] * len(operands),
        out_specs=(spec,) * len(outs),
        scratch_shapes=scratch,
        compiler_params=pltpu.CompilerParams(
            collective_id=0, has_side_effects=True, vmem_limit_bytes=36 * 2**20
        ),
        name="outer_mean",
    )(*operands)
    edge, cols, rows, g_fin, g_wl, g_wr, g_bias = copy_out(results)
    return (
        edge.reshape(own, own, wide),
        from_tiles(cols, depth, own),
        from_tiles(rows, depth, own),
        g_wl.T,
        g_wr.T,
        g_fin,
        g_bias.reshape(wide),
    )


def solution(mesh):
    parts = P("seq", "res", None)
    in_specs = (parts, parts, P(), P(), P(), P(), parts)
    out_specs = (parts, parts, parts, P(), P(), P(), P())
    return jax.shard_map(body, mesh=mesh, in_specs=in_specs, out_specs=out_specs, check_vma=False)
```

```python
import functools

import jax
import jax.numpy as jnp
from jax import lax
from jax.experimental import pallas as pl
from jax.experimental.pallas import tpu as pltpu
from jax.sharding import PartitionSpec as P

EPS = 1e-05
RES = (2, 4, 2)
SEMS = 78
F32 = jnp.float32
BF16 = jnp.bfloat16
MESH = pl.DeviceIdType.MESH
NN = (((1,), (0,)), ((), ()))
NT = (((1,), (1,)), ((), ()))


def mm(a, b, dims=NN):
    return lax.dot_general(a, b, dims, preferred_element_type=F32)


def split(x):
    high = x.astype(BF16)
    return high, (x - high.astype(F32)).astype(BF16)


def mm3(a, b, dims=NN):
    rows = a[0].shape[0]
    both = mm(jnp.concatenate(a, axis=0), b[0], dims)
    return both[:rows] + (both[rows:] + mm(a[0], b[1], dims))


class Group:
    def __init__(self, size, me, id_of, peer=None):
        self.size = size
        self.me = me
        self.id_of = id_of
        self.plain = lambda n: lax.rem(me + 1 + n, size)
        self.peer = peer or self.plain

    def each(self, act, plain=False):
        def one(n, _):
            act(self.plain(n) if plain else self.peer(n))
            return 0

        if self.size > 1:
            lax.fori_loop(0, self.size - 1, one, 0)


class Semaphores:
    def __init__(self, ref):
        self.ref = ref
        self.used = 0

    def take(self, count=1):
        self.used += count
        return self.used - count


class Exchange:
    def __init__(self, group, sems, src_of, dst_of, bulk=None, single=False, share=None):
        self.group = group
        self.sems = sems
        self.src_of = src_of
        self.dst_of = dst_of
        self.bulk = bulk
        self.single = single
        if share is None:
            self.sent = sems.take()
            self.came = sems.take(group.size if single else 1)
        else:
            self.sent = share.sent
            self.came = sems.take(group.size) if single else share.came

    def describe(self, src, dst, slot, peer):
        return pltpu.make_async_remote_copy(
            src_ref=src,
            dst_ref=dst,
            send_sem=self.sems.ref.at[self.sent],
            recv_sem=self.sems.ref.at[self.came + slot if self.single else self.came],
            device_id=self.group.id_of(peer),
            device_id_type=MESH,
        )

    def start_to(self, peer):
        me = self.group.me
        self.describe(self.src_of(peer), self.dst_of(me), me, peer).start()

    def start(self):
        self.group.each(self.start_to)

    def wait_from(self, peer):
        self.describe(self.src_of(peer), self.dst_of(peer), peer, peer).wait_recv()

    def wait_recv(self):
        if self.group.size > 1:
            self.describe(self.bulk, self.bulk, 0, self.group.me).wait_recv()

    def wait_send(self):
        if self.group.size > 1:
            self.describe(self.bulk, self.bulk, 0, self.group.me).wait_send()


def signal_peers(groups):
    barrier = pltpu.get_barrier_semaphore()
    for group in groups:

        def signal(peer, group=group):
            pl.semaphore_signal(
                barrier, inc=1, device_id=group.id_of(peer), device_id_type=MESH
            )

        group.each(signal, plain=True)


def wait_peers(groups):
    total = sum(group.size - 1 for group in groups)
    pl.semaphore_wait(pltpu.get_barrier_semaphore(), total)


def block(index, rows):
    return pl.ds(pl.multiple_of(index * rows, rows), rows)


def norm_rows(x_ref, normed, inverse, own, depth):
    def one(i, _):
        x = jnp.concatenate(
            [x_ref[pl.ds(i + p * own, depth, stride=2 * own), :] for p in range(2)], axis=1
        )
        centred = x - jnp.mean(x, axis=-1, keepdims=True)
        inv = lax.rsqrt(jnp.mean(centred * centred, axis=-1, keepdims=True) + EPS)
        normed[block(i, depth), :] = centred * inv
        inverse[block(i, depth), :] = inv
        return 0

    lax.fori_loop(0, own, one, 0)


def norm_back(upstream, normed, inverse, out_ref, own, depth):
    for i in range(own):
        rows = slice(i * depth, (i + 1) * depth)
        u = upstream[rows, :]
        y = normed[rows, :]
        first = jnp.mean(u, axis=-1, keepdims=True)
        second = jnp.mean(u * y, axis=-1, keepdims=True)
        g = inverse[rows, :] * (u - first - y * second)
        for p in range(2):
            lanes = slice(p * 128, (p + 1) * 128)
            out_ref[pl.ds(i + p * own, depth, stride=2 * own), :] = g[:, lanes]


def kernel(
    src_in, tgt_in, wl_in, wr_in, fin_in, bias_in, cot_in,
    edge_res, cols_res, rows_res, fin_res, gl_res, gr_res, gb_res,
    src, tgt, wl_t, wr_t, fin, bias, cot,
    edge_out, cols_out, rows_out, fin_out, gl_out, gr_out, gb_out,
    xs, xs_inv, xt, xt_inv, turn, left_blk, left_all, left_hl, lt_h, lt_l,
    cot_blk, cot_all, cot_hl, cot_t, fin_h, fin_l, b_h, b_l,
    gls_part, gls_c, gls_1, gls_x, gls_2, gls_y,
    edge_part, edge_in, da_h, da_l, db_h, db_l, acc64, acc32, grs_ref, up,
    big, big_c, big_1, big_x, small, small_x,
    big_2, big_far, big_3, big_s, big_r, small_2, small_far, small_3, small_s, small_r,
    in_sem, out_sem, comm_sem,
    *, own, depth, hid, wide,
):
    nr = lax.axis_size("res")
    ns = lax.axis_size("seq")
    res_me = lax.axis_index("res")
    seq_me = lax.axis_index("seq")
    scale = 1.0 / (depth * ns)
    pairs = hid // 2
    half = depth
    tile = 2 * depth
    full = own * nr
    yn, xn, cn = RES
    core = lax.rem(res_me, cn)
    ex = lax.rem(res_me // cn, xn)
    wy = res_me // (cn * xn)
    others = [lax.rem(wy + d, yn) for d in range(1, yn)]
    near = sorted(range(1, xn), key=lambda d: min(d, xn - d))
    steps = [lax.rem(ex + d, xn) for d in near]

    def res_id(y, x, c):
        return (y * xn + x) * cn + c

    g_core = Group(cn, core, lambda m: {"res": res_id(wy, ex, m)})
    g_x = Group(xn, ex, lambda m: {"res": res_id(wy, m, core)})
    g_y = Group(yn, wy, lambda m: {"res": res_id(m, ex, core)})
    zn = ns // 2
    zed = seq_me // 2

    def seq_peer(k, flip):
        turn_z = (1 - 2 * lax.rem(k, 2)) * ((k + 1) // 2)
        return lax.rem(zed + zn + zn // 2 + turn_z, zn) * 2 + lax.rem(seq_me + flip, 2)

    def far_peer(n):
        rest = lax.rem(n + 1, 2 * yn)
        return lax.rem(wy + rest // 2, yn) * ns + seq_peer(n // (2 * yn), lax.rem(rest, 2))

    g_seq = Group(ns, seq_me, lambda m: {"seq": m})
    g_far = Group(
        yn * ns,
        wy * ns + seq_me,
        lambda m: {"res": res_id(m // ns, ex, core), "seq": lax.rem(m, ns)},
        far_peer,
    )
    g_xc = Group(
        xn * cn, ex * cn + core, lambda m: {"res": res_id(wy, m // cn, lax.rem(m, cn))}
    )
    greeted = (g_xc, g_far)
    sems = Semaphores(comm_sem)
    loads = [
        pltpu.make_async_copy(a, b, in_sem.at[n])
        for n, (a, b) in enumerate(
            zip(
                (src_in, wl_in, cot_in, tgt_in, wr_in, fin_in, bias_in),
                (src, wl_t, cot, tgt, wr_t, fin, bias),
            )
        )
    ]
    for load in loads:
        load.start()
    signal_peers(greeted)
    for load in loads[:3]:
        load.wait()

    norm_rows(src, xs, xs_inv, own, depth)
    wl_ts = split(wl_t[...])
    left_t = mm3(wl_ts, split(xs[...]), NT)
    low = lax.broadcasted_iota(jnp.int32, (hid, tile), 1) < half
    for u in range(own // 2):
        a = left_t[:, u * tile : (u + 1) * tile]
        b = pltpu.roll(a, half, 1)
        turn[2 * u * hid : (2 * u + 1) * hid, :] = jnp.where(low, a, b)
        turn[(2 * u + 1) * hid : (2 * u + 2) * hid, :] = jnp.where(low, b, a)
    low8 = lax.broadcasted_iota(jnp.int32, (own, tile), 1) < half
    for t in range(pairs):
        even = turn[pl.ds(2 * t, own, stride=hid), :]
        odd = turn[pl.ds(2 * t + 1, own, stride=hid), :]
        left_blk[:, t * tile : (t + 1) * tile] = jnp.where(low8, even, odd)
    for j in range(own):
        cot_blk[:, j * wide : (j + 1) * wide] = cot[pl.ds(j, own, stride=own), :]

    wait_peers(greeted)

    def left_at(y, x, c):
        return left_all.at[block(res_id(y, x, c), own)]

    x_cot = Exchange(
        g_seq, sems, lambda t: cot_blk, lambda k: cot_all.at[block(k, own)],
        cot_all.at[: (ns - 1) * own],
    )
    left_xs = Exchange(
        g_x, sems, lambda t: left_blk, lambda k: left_at(wy, k, core),
        left_all.at[: (xn - 1) * own], single=True,
    )
    left_ys = Exchange(
        g_y, sems, lambda t: left_blk, lambda k: left_at(k, ex, core),
        left_all.at[: (yn - 1) * own],
    )
    left_far = [
        Exchange(
            g_x, sems, lambda t, y=y: left_at(y, ex, core), lambda k, y=y: left_at(y, k, core),
            left_all.at[: (xn - 1) * own], single=True,
        )
        for y in others
    ]
    left_own = Exchange(
        g_core, sems, lambda t: left_blk, lambda k: left_at(wy, ex, k),
        left_all.at[: yn * xn * own],
    )

    def to_core(y, x):
        return Exchange(
            g_core, sems, lambda t: left_at(y, x, core), lambda k: left_at(y, x, k), share=left_own
        )

    left_mates = [to_core(y, ex) for y in others]
    left_mates_x = [to_core(wy, x) for x in steps]
    left_mates_far = [[to_core(y, x) for x in steps] for y in others]
    left_ys.start()
    left_xs.start()
    left_own.start()
    x_cot.start()
    cot_all[block(seq_me, own), :] = cot_blk[...]
    left_all[block(res_me, own), :] = left_blk[...]

    for load in loads[3:]:
        load.wait()
    norm_rows(tgt, xt, xt_inv, own, depth)
    wr_ts = split(wr_t[...])
    right = mm3(split(xt[...]), wr_ts, NT) * scale
    right_h, right_l = split(right)
    right_k = jnp.concatenate([right_h, right_h, right_l], axis=1)
    rt_h, rt_l = split(right.T)
    left_ys.wait_recv()
    for far, mate in zip(left_far, left_mates):
        far.start()
        mate.start()
    rt_hl = jnp.concatenate([rt_h, rt_l], axis=0)
    fh, fl = split(fin[...])
    fin_h[...] = fh
    fin_l[...] = fl

    def make_b(hp, _):
        def stacked(p):
            rows = block(2 * hp + p, hid)
            return jnp.concatenate([fin_h[rows, :], fin_l[rows, :], fin_h[rows, :]], axis=0)

        weights = jnp.concatenate([stacked(0), stacked(1)], axis=1)
        for j in range(own):
            val = mm(right_k[j * depth : (j + 1) * depth], weights)
            vh, vl = split(val)
            for p in range(2):
                rows = block(2 * hp + p, depth)
                lanes = slice(p * wide, (p + 1) * wide)
                b_h[rows, j * wide : (j + 1) * wide] = vh[:, lanes]
                b_l[rows, j * wide : (j + 1) * wide] = vl[:, lanes]
        return 0

    lax.fori_loop(0, pairs, make_b, 0)
    for x, mate in zip(steps, left_mates_x):
        left_xs.wait_from(x)
        mate.start()
    for far, mates in zip(left_far, left_mates_far):
        for x, mate in zip(steps, mates):
            far.wait_from(x)
            mate.start()

    x_cot.wait_recv()
    ch, cl = split(cot_all[...])
    rows_all = ns * own
    cot_hl[:rows_all, :] = ch
    cot_hl[rows_all:, :] = cl
    cot_h = cot_hl.at[:rows_all]
    cot_l = cot_hl.at[rows_all:]
    for j in range(own):
        rows = slice(j * wide, (j + 1) * wide)
        th, tl = split(cot_all[:, rows].T)
        cot_t[rows, :rows_all] = th
        cot_t[rows, rows_all:] = tl

    def make_gls(n, _):
        rows = block(n, 8 * tile)
        y = mm(b_h[rows, :], cot_t[...])
        val = y[:, :rows_all] + (y[:, rows_all:] + mm(b_l[rows, :], cot_t[:, :rows_all]))
        gls_part[:, block(n, 8 * tile)] = val.T
        return 0

    lax.fori_loop(0, hid * depth // (8 * tile), make_gls, 0)

    def gls_at(y, x, c):
        return gls_part.at[block(res_id(y, x, c), own)]

    ys = [wy, *others]
    xs_of = [ex, *steps]
    order = [(dy, dx) for dx in [*range(xn - 1, 0, -1), 0] for dy in [*range(1, yn), 0]]
    mate_gls = {}
    first_gls = None
    for dy, dx in order:
        mate_gls[dy, dx] = Exchange(
            g_core,
            sems,
            lambda t, y=ys[dy], x=xs_of[dx]: gls_at(y, x, t),
            lambda k, y=ys[dy], x=xs_of[dx]: gls_c.at[y * xn + x],
            gls_c,
            single=True,
            share=first_gls,
        )
        first_gls = first_gls or mate_gls[dy, dx]
        mate_gls[dy, dx].start()
    x_gls = [
        Exchange(
            g_x, sems, lambda t, y=y: gls_1.at[y * xn + t], lambda k, y=y: gls_x.at[y * xn + k],
            gls_x.at[: xn - 1],
        )
        for y in ys
    ]

    def pass_gls(some):
        for dy, dx in some:
            if cn > 1:
                mate_gls[dy, dx].wait_from(cn - 1 - core)
            at = ys[dy] * xn + xs_of[dx]
            mine = gls_at(ys[dy], xs_of[dx], core)[...]
            gls_1[at] = mine + gls_c[at] if cn > 1 else mine
            if dx:
                x_gls[dy].start_to(xs_of[dx])

    left_own.wait_recv()
    for t in range(pairs):
        lanes = slice(t * tile, (t + 1) * tile)
        val = left_all[:, lanes]
        lh, ll = split(val)
        left_hl[:full, lanes] = lh
        left_hl[full:, lanes] = ll
        th, tl = split(val.T)
        lt_h[lanes, :] = th
        lt_l[lanes, :] = tl

    tiles = own // 2
    for n in range(tiles):
        cols = slice(2 * n * wide, 2 * (n + 1) * wide)
        y = mm(left_hl[...], b_h[:, cols])
        edge_part[:, cols] = y[:full] + (y[full:] + mm(left_hl[:full], b_l[:, cols]))
    x_edge = Exchange(
        g_seq, sems, lambda t: edge_part.at[block(t, own)], lambda k: edge_in.at[k],
        edge_in.at[: ns - 1],
    )
    x_edge.start()
    edge_in[seq_me] = edge_part[block(seq_me, own), :]

    acc64[...] = jnp.zeros_like(acc64)
    acc32[...] = jnp.zeros_like(acc32)

    def make_db(q, dst_h, dst_l):
        a_h = lt_h[block(q, 2 * tile), :]
        a_hl = jnp.concatenate([a_h, lt_l[block(q, 2 * tile), :]], axis=1)
        for jj in range(own // 2):
            cols = slice(2 * jj * wide, 2 * (jj + 1) * wide)
            c_h = cot_h[:, cols]
            val = mm(a_hl, jnp.concatenate([c_h, c_h], axis=0)) + mm(a_h, cot_l[:, cols])
            vh, vl = split(val)
            for r in range(2):
                rows = slice((2 * jj + r) * depth, (2 * jj + r + 1) * depth)
                lanes = slice(r * wide, (r + 1) * wide)
                for p in range(4):
                    part = slice(p * depth, (p + 1) * depth)
                    dst_h[rows, p * wide : (p + 1) * wide] = vh[part, lanes]
                    dst_l[rows, p * wide : (p + 1) * wide] = vl[part, lanes]

    def use_db(q, src_h, src_l):
        dh = src_h[...]
        dl = src_l[...]
        y = mm(rt_hl, dh)
        grad = y[:hid, :] + (y[hid:, :] + mm(rt_h, dl))
        big[:, q, :, :] = grad.reshape(hid, 1, 4 * wide)

        def flat(ref):
            return jnp.concatenate([ref[block(4 * q + p, hid), :] for p in range(4)], axis=1)

        f_h = flat(fin_h)
        acc64[...] += mm(dh, jnp.concatenate([f_h, flat(fin_l)], axis=0), NT)
        acc32[...] += mm(dl, f_h, NT)

    def two_db(t, _):
        make_db(2 * t + 1, db_h, db_l)
        use_db(2 * t, da_h, da_l)
        make_db(2 * t + 2, da_h, da_l)
        use_db(2 * t + 1, db_h, db_l)
        return 0

    per_c = hid // cn
    per = per_c // xn

    def start_core(whole, mine, quads):
        out = Exchange(
            g_core, sems, lambda t: whole.at[pl.ds(t * per_c, per_c), quads],
            lambda k: mine.at[:, quads], mine.at[:, quads],
        )
        out.start()
        return out

    def fold_core(exchange, whole, other, total, quads):
        exchange.wait_recv()
        if cn > 1:
            total[:, quads] = whole[pl.ds(core * per_c, per_c), quads] + other[:, quads]
        else:
            total[:, quads] = whole[:, quads]

    def start_x(total, arrived, quads):
        out = Exchange(
            g_x, sems, lambda t: total.at[pl.ds(t * per, per), quads],
            lambda k: arrived.at[k, :, quads], arrived.at[: xn - 1, :, quads],
        )
        out.start()
        arrived[ex, :, quads] = total[pl.ds(ex * per, per), quads]
        return out

    halves = [pl.ds(0, 4), pl.ds(4, 4)]
    every = pl.ds(0, 8)
    quads = hid // 4
    pass_gls(order[:1])
    make_db(0, da_h, da_l)
    pass_gls(order[1:2])
    for t in range(quads // 2 - 1):
        lax.fori_loop(t, t + 1, two_db, 0)
        pass_gls(order[2 * t + 2 : 2 * t + 4])
        if t == quads // 4 - 1:
            core_big = [start_core(big, big_c, halves[0])]
    make_db(quads - 1, db_h, db_l)
    use_db(quads - 2, da_h, da_l)
    use_db(quads - 1, db_h, db_l)
    core_big.append(start_core(big, big_c, halves[1]))
    fold_core(core_big[0], big, big_c, big_1, halves[0])
    x_big = [start_x(big_1, big_x, halves[0])]

    both = acc64[...]
    grs = (both[:, :hid] + both[:, hid:] + acc32[...]) * scale
    xts = split(xt[...])
    gr_t = mm3(split(grs.T), xts)
    gb = jnp.sum(cot[...], axis=0, keepdims=True)
    for h in range(2):
        small[:, 2 + h, :, :] = gr_t[:, h * wide : (h + 1) * wide].reshape(hid, 1, wide)
    small[:, 4, :, :] = jnp.broadcast_to(gb, (hid, wide)).reshape(hid, 1, wide)
    for h in range(5, 8):
        small[:, h, :, :] = jnp.zeros((hid, 1, wide), F32)

    def fold_x(y, arriving):
        arriving.wait_recv()
        total = gls_1[y * xn + ex]
        for x in steps:
            total = total + gls_x[y * xn + x]
        return total

    y_gls = Exchange(
        g_y, sems, lambda t: gls_2.at[t], lambda k: gls_y.at[k], gls_y.at[: yn - 1]
    )
    for y, arriving in zip(others, x_gls[1:]):
        gls_2[y] = fold_x(y, arriving)
        y_gls.start_to(y)
    gls = fold_x(wy, x_gls[0])
    fold_core(core_big[1], big, big_c, big_1, halves[1])
    x_big.append(start_x(big_1, big_x, halves[1]))
    stores = []

    def store(value, result):
        stores.append(pltpu.make_async_copy(value, result, out_sem.at[len(stores)]))
        stores[-1].start()

    up[...] = mm3(split(grs), wr_ts)
    norm_back(up, xt, xt_inv, cols_out, own, depth)
    store(cols_out, cols_res)
    y_gls.wait_recv()
    for y in others:
        gls = gls + gls_y[y]
    for t in range(pairs):
        v = gls[:, t * tile : (t + 1) * tile]
        turn[pl.ds(2 * t, own, stride=hid), :] = v
        turn[pl.ds(2 * t + 1, own, stride=hid), :] = pltpu.roll(v, half, 1)
    parts = []
    for u in range(own // 2):
        a = turn[2 * u * hid : (2 * u + 1) * hid, :]
        b = turn[(2 * u + 1) * hid : (2 * u + 2) * hid, :]
        parts.append(jnp.where(low, a, pltpu.roll(b, half, 1)))
    gls_t = jnp.concatenate(parts, axis=1)
    gl_t = mm3(split(gls_t), split(xs[...]))
    for h in range(2):
        small[:, h, :, :] = gl_t[:, h * wide : (h + 1) * wide].reshape(hid, 1, wide)
    def small_at(m):
        return small.at[pl.ds(lax.rem(m, cn) * per_c + (m // cn) * per, per)]

    xc_small = Exchange(
        g_xc, sems, small_at, lambda k: small_x.at[k], small_x.at[: xn * cn - 1]
    )
    xc_small.start()
    small_x[g_xc.me] = small_at(g_xc.me)[...]

    span_rows, span = far_chunk(per, g_far.size)
    groups = 8 // span

    def at(ref, t):
        return ref.at[
            pl.ds((t // groups) * span_rows, span_rows), pl.ds(lax.rem(t, groups) * span, span)
        ]

    def start_far(exchanges, arrived, total, parts):
        for exchange in exchanges:
            exchange.wait_recv()
        total[...] = jnp.sum(arrived[...], axis=0)
        out = Exchange(
            g_far, sems, lambda t: at(total, t), lambda k: parts.at[k], parts.at[: g_far.size - 1]
        )
        out.start()
        parts[g_far.me] = at(total, g_far.me)[...]
        return out

    def start_back(exchange, parts, mine, whole):
        exchange.wait_recv()
        mine[...] = jnp.sum(parts[...], axis=0)
        out = Exchange(
            g_far, sems, lambda t: mine, lambda k: at(whole, k), parts.at[: g_far.size - 1]
        )
        out.start()
        at(whole, g_far.me)[...] = mine[...]
        return out

    def red_at(red, c, x, q):
        return red.at[pl.ds(c * per_c + x * per, per), q]

    def start_wide(exchange, whole, red, parts):
        exchange.wait_recv()
        outs = []
        for q in parts:
            outs.append(
                Exchange(
                    g_x, sems, lambda t, q=q: whole.at[:, q],
                    lambda k, q=q: red_at(red, core, k, q),
                    red.at[: (xn - 1) * per, q], single=True,
                )
            )
            outs[-1].start()
        mate = Exchange(
            g_core, sems, lambda t: whole, lambda k: red_at(red, k, ex, every), red.at[: xn * per]
        )
        mate.start()
        red_at(red, core, ex, every)[...] = whole[...]
        return outs, mate

    def start_mates(outs, mate, red, parts):
        for out, q in zip(outs, parts):
            for x in steps:
                out.wait_from(x)
                Exchange(
                    g_core,
                    sems,
                    lambda t, x=x, q=q: red_at(red, core, x, q),
                    lambda k, x=x, q=q: red_at(red, k, x, q),
                    share=mate,
                ).start()

    far_big = start_far(x_big, big_x, big_2, big_far)
    up[...] = mm3(split(gls_t.T), wl_ts)
    norm_back(up, xs, xs_inv, rows_out, own, depth)
    store(rows_out, rows_res)

    x_edge.wait_recv()
    edge = edge_in[0]
    for k in range(1, ns):
        edge = edge + edge_in[k]
    for j in range(own):
        edge_out[pl.ds(j, own, stride=own), :] = edge[:, j * wide : (j + 1) * wide] + bias[...]
    store(edge_out, edge_res)

    far_small = start_far([xc_small], small_x, small_2, small_far)
    back_big = start_back(far_big, big_far, big_3, big_s)
    for sent in (
        x_cot, left_xs, left_ys, left_own, *left_far, first_gls, *x_gls, y_gls, x_edge,
        *core_big, xc_small, *x_big, far_big,
    ):
        sent.wait_send()
    back_small = start_back(far_small, small_far, small_3, small_s)
    wide_big, mate_big = start_wide(back_big, big_s, big_r, halves)
    start_mates(wide_big, mate_big, big_r, halves)
    wide_small, mate_small = start_wide(back_small, small_s, small_r, [every])
    start_mates(wide_small, mate_small, small_r, [every])
    mate_big.wait_recv()
    for h in range(hid):
        fin_out[h * hid : (h + 1) * hid, :] = big_r[
            :, h // 4, :, (h % 4) * wide : (h % 4 + 1) * wide
        ].reshape(hid, wide)
    store(fin_out, fin_res)
    for sent in (far_small, back_big, back_small, *wide_big, mate_big):
        sent.wait_send()
    mate_small.wait_recv()
    for h in range(2):
        lanes = slice(h * wide, (h + 1) * wide)
        gl_out[:, lanes] = small_r[:, h].reshape(hid, wide)
        gr_out[:, lanes] = small_r[:, 2 + h].reshape(hid, wide)
    gb_out[...] = small_r[0, 4]
    store(gl_out, gl_res)
    store(gr_out, gr_res)
    store(gb_out, gb_res)
    for sent in (*wide_small, mate_small):
        sent.wait_send()
    for put in stores:
        put.wait()
    assert sems.used <= SEMS, sems.used


def copy_kernel(*refs):
    count = (len(refs) - 1) // 2
    puts = [
        pltpu.make_async_copy(a, b, refs[-1].at[n])
        for n, (a, b) in enumerate(zip(refs[:count], refs[count : 2 * count]))
    ]
    for put in puts:
        put.start()
    for put in puts:
        put.wait()


def copy_out(arrays):
    return pl.pallas_call(
        copy_kernel,
        out_shape=tuple(jax.ShapeDtypeStruct(a.shape, a.dtype) for a in arrays),
        in_specs=[pl.BlockSpec(memory_space=pl.ANY)] * len(arrays),
        out_specs=(pl.BlockSpec(memory_space=pltpu.MemorySpace.HBM),) * len(arrays),
        scratch_shapes=[pltpu.SemaphoreType.DMA((len(arrays),))],
        compiler_params=pltpu.CompilerParams(vmem_limit_bytes=2**20),
        name="copy_out",
    )(*arrays)


def far_chunk(per, members):
    quads = max(1, 8 // members)
    return per * 8 // (members * quads), quads


def to_tiles(x):
    depth, own, chan = x.shape
    return x.reshape(depth, own, 2, chan // 2).swapaxes(1, 2).reshape(-1, chan // 2)


def from_tiles(x, depth, own):
    return x.reshape(depth, 2, own, -1).swapaxes(1, 2).reshape(depth, own, -1)


def body(tgt, src, wl, wr, fin, bias, cot):
    ns = lax.axis_size("seq")
    nr = lax.axis_size("res")
    depth, own, chan = src.shape
    hid = wl.shape[1]
    wide = fin.shape[1]
    flat = own * depth
    yn, xn, cn = RES
    per_c = hid // cn
    per = per_c // xn
    far = yn * ns
    few, quads = far_chunk(per, far)
    v = pltpu.VMEM
    k = hid * depth
    n = own * wide
    operands = (
        to_tiles(src), to_tiles(tgt), wl.T, wr.T, fin,
        bias.reshape(1, wide), cot.reshape(own * own, wide),
    )
    outs = (
        jax.ShapeDtypeStruct((own * own, wide), F32),
        jax.ShapeDtypeStruct((2 * flat, 128), F32),
        jax.ShapeDtypeStruct((2 * flat, 128), F32),
        jax.ShapeDtypeStruct((hid * hid, wide), F32),
        jax.ShapeDtypeStruct((hid, chan), F32),
        jax.ShapeDtypeStruct((hid, chan), F32),
        jax.ShapeDtypeStruct((1, wide), F32),
    )
    scratch = [v(a.shape, F32) for a in (*operands, *outs)] + [
        v((flat, chan), F32), v((flat, 1), F32), v((flat, chan), F32), v((flat, 1), F32),
        v((own * hid, 2 * depth), F32), v((own, k), F32), v((nr * own, k), F32),
        v((2 * nr * own, k), BF16), v((k, nr * own), BF16), v((k, nr * own), BF16),
        v((own, n), F32), v((ns * own, n), F32), v((2 * ns * own, n), BF16), v((n, 2 * ns * own), BF16),
        v((hid * hid, wide), BF16), v((hid * hid, wide), BF16), v((k, n), BF16), v((k, n), BF16),
        v((nr * own, k), F32), v((yn * xn, own, k), F32), v((yn * xn, own, k), F32),
        v((yn * xn, own, k), F32), v((yn, own, k), F32), v((yn, own, k), F32),
        v((ns * own, n), F32), v((ns, own, n), F32),
        v((flat, 4 * wide), BF16), v((flat, 4 * wide), BF16), v((flat, 4 * wide), BF16),
        v((flat, 4 * wide), BF16), v((flat, 2 * hid), F32), v((flat, hid), F32),
        v((flat, hid), F32), v((flat, chan), F32),
        v((hid, 8, 1, 4 * wide), F32), v((per_c, 8, 1, 4 * wide), F32),
        v((per_c, 8, 1, 4 * wide), F32), v((xn, per, 8, 1, 4 * wide), F32),
        v((hid, 8, 1, wide), F32), v((xn * cn, per, 8, 1, wide), F32),
    ]
    for lanes in (4 * wide, wide):
        scratch += [
            v((per, 8, 1, lanes), F32), v((far, few, quads, 1, lanes), F32),
            v((few, quads, 1, lanes), F32), v((per, 8, 1, lanes), F32),
            v((hid, 8, 1, lanes), F32),
        ]
    scratch += [
        pltpu.SemaphoreType.DMA((len(operands),)), pltpu.SemaphoreType.DMA((len(outs),)),
        pltpu.SemaphoreType.DMA((SEMS,)),
    ]
    spec = pl.BlockSpec(memory_space=pl.ANY)
    operands = tuple(pltpu.with_memory_space_constraint(a, pltpu.MemorySpace.HBM) for a in operands)
    results = pl.pallas_call(
        functools.partial(kernel, own=own, depth=depth, hid=hid, wide=wide),
        out_shape=outs,
        in_specs=[pl.BlockSpec(memory_space=pltpu.MemorySpace.HBM)] * len(operands),
        out_specs=(spec,) * len(outs),
        scratch_shapes=scratch,
        compiler_params=pltpu.CompilerParams(
            collective_id=0, has_side_effects=True, vmem_limit_bytes=36 * 2**20
        ),
        name="outer_mean",
    )(*operands)
    edge, cols, rows, g_fin, g_wl, g_wr, g_bias = copy_out(results)
    return (
        edge.reshape(own, own, wide),
        from_tiles(cols, depth, own),
        from_tiles(rows, depth, own),
        g_wl.T,
        g_wr.T,
        g_fin,
        g_bias.reshape(wide),
    )


def solution(mesh):
    parts = P("seq", "res", None)
    in_specs = (parts, parts, P(), P(), P(), P(), parts)
    out_specs = (parts, parts, parts, P(), P(), P(), P())
    return jax.shard_map(body, mesh=mesh, in_specs=in_specs, out_specs=out_specs, check_vma=False)
```
